32 devices in a mesh: layer: 4 (over y, x), head: 4 (over z), qblk: 2 (over core).
Axes of the slice: x: 2, y: 2, z: 4, core: 2. Of those that a mesh axis runs over, the one named last changes fastest.
Arguments:
- inputs: bfloat16 [384, 5120], P(('layer', 'qblk')), may hold values from -6 to 6
- key_weight: bfloat16 [5120, 512], P(None, 'head'), may hold values from -0.078125 to 0.078125
- value_weight: bfloat16 [5120, 512], P(None, 'head'), may hold values from -0.078125 to 0.078125
- queries: bfloat16 [4, 384, 2560], P('layer', 'qblk', 'head'), may hold values from -192 to 192
- output_cotangent: bfloat16 [4, 384, 2560], P('layer', 'qblk', 'head'), may hold values from -6 to 6
- documents: int32 [384], replicated, may hold values from 0 to 5, never falling along the last dimension, each value on 1 to 192 neighbouring positions
Outputs:
- query_gradient: bfloat16 [4, 384, 2560], P('layer', 'qblk', 'head')
- input_gradient: bfloat16 [384, 5120], P(('layer', 'qblk'), 'head')
The draws below stay inside these ranges and needn't reach their ends.
Inputs may be any that keep to these rules, and one draw needn't show every extreme that they name: `documents`: never falls along the sequence; every document has 1 to 192 positions, and one has exactly 192.
All inputs are finite; a program needn't handle non-finite values.
Results may differ from the reference program's by a relative error of at most 0.018.
The reference program's roundings to bfloat16 on the way count: a program that leaves them out, or rounds other values in their place, can miss the bound.
Values may be sent and summed in bfloat16 or wider, within the bound.
A program may use at most 64 MiB of HBM per device.

```python
import math
import jax
import jax.numpy as jnp
import numpy as np
from jax import lax

D = 5120
HD = 128
GROUP = 5
DOCS = 6
KVH = 4
QH = 20
LAYERS = 4
SEQ = 384


def draw_queries(key, part):
    base_key = jax.random.fold_in(jax.random.fold_in(key, 17), 0)
    values = jnp.clip(jax.random.normal(base_key, (LAYERS, SEQ, QH * HD), jnp.float32), -8.0, 8.0)
    return values.astype(jnp.bfloat16)


def levels(rng, extent, pieces, least, largest):
    gain, own = 1.0, jax.random.fold_in(rng, 6)
    for position, parts in pieces:
        draws = jnp.exp(jax.random.uniform(jax.random.fold_in(own, position), (parts,), jnp.float32, least / len(pieces), largest / len(pieces)))
        gain = gain * jnp.repeat(draws, extent[position] // parts).reshape([-1 if axis == position else 1 for axis in range(len(extent))])
    return gain


def profile(number_of, total, limit, slope):
    loads = [(1 << 20) // math.isqrt(rank ** slope) + 1 for rank in range(2, number_of + 1)]
    rest, counts = total - limit - (number_of - 1), [1] * (number_of - 1)
    while rest > 0:
        free = [i for i in range(number_of - 1) if counts[i] < limit]
        mass, budget = sum([loads[i] for i in free]), rest
        for i in free:
            extra = min(limit - counts[i], max(1, budget * loads[i] // mass), rest)
            counts[i] = counts[i] + extra
            rest = rest - extra
    return np.array([limit] + counts)


def uneven_parts(rng, count, total, reach, skew):
    if count == 2:
        one = jax.random.randint(rng, (), max(1, total - reach), min(reach, total - 1) + 1)
        return jnp.stack([one, total - one])
    tallies = jnp.asarray(profile(count, total, reach, skew), jnp.int32)
    pairs = (count - 1) // 2
    source_of, receiver = tallies[1:1 + 2 * pairs:2], tallies[2:2 + 2 * pairs:2]
    margin = jnp.minimum(source_of - 1, reach - receiver)
    shifted = jax.random.randint(jax.random.fold_in(rng, 1), (pairs,), 0, 1 << 20) % (margin + 1)
    tallies = tallies.at[1:1 + 2 * pairs:2].set(source_of - shifted).at[2:2 + 2 * pairs:2].set(receiver + shifted)
    return tallies[jax.random.permutation(jax.random.fold_in(rng, 2), count)]


def noise(key, dims, deviation, limit, pieces=(), kind=jnp.bfloat16):
    result = jax.random.normal(key, dims, jnp.float32) * deviation
    if len(pieces) > 0:
        result = levels(key, dims, pieces, -0.22, 0.18) * result
    return jnp.clip(result, min=-limit, max=limit).astype(kind)


def setup_inputs(seed: int = 0) -> dict:
    key_of = jax.random.split(jax.random.key(seed), 7)
    return {
        "inputs": noise(key_of[0], (SEQ, D), 1.0, 6.0, ((0, 8),)),
        "key_weight": noise(key_of[1], (D, KVH * HD), D ** -0.5, 0.078125, ((1, 4),)),
        "value_weight": noise(key_of[2], (D, KVH * HD), D ** -0.5, 0.078125, ((1, 4),)),
        "queries": draw_queries(jax.random.fold_in(key_of[6], 71), 0),
        "output_cotangent": noise(key_of[4], (LAYERS, SEQ, QH * HD), 1.0, 6.0, ((0, 4), (1, 2), (2, 4))),
        "documents": jnp.searchsorted(jnp.cumsum(uneven_parts(key_of[5], DOCS, SEQ, SEQ // 2, 1)), jnp.arange(SEQ), side="right").astype(jnp.int32),
    }


def backward_one(query, key_tile, value_tile, cotangent, allowed):
    scaling = HD ** -0.5
    query_float = query.astype(jnp.float32)
    key_float = key_tile.astype(jnp.float32)
    value_float = value_tile.astype(jnp.float32)
    cot_float = cotangent.astype(jnp.float32)
    logits = jnp.einsum('qgd,kd->gqk', query_float, key_float) * scaling
    logits = jnp.where(allowed[None], logits, -1e30)
    row_max = jnp.max(logits, -1, keepdims=True)
    row_total = jnp.sum(jnp.where(allowed[None], jnp.exp(logits - row_max), 0.0), -1, keepdims=True)
    log_total = row_max + jnp.log(row_total)
    probability = jnp.where(allowed[None], jnp.exp(logits - log_total), 0.0)
    prob_grad = jnp.einsum('qgd,kd->gqk', cot_float, value_float)
    row_delta = jnp.sum(probability * prob_grad, -1, keepdims=True)
    score_grad = probability * (prob_grad - row_delta)
    prob_short = lax.optimization_barrier(probability.astype(jnp.bfloat16)).astype(jnp.float32)
    score_short = lax.optimization_barrier(score_grad.astype(jnp.bfloat16)).astype(jnp.float32)
    value_grad = jnp.einsum('gqk,qgd->kd', prob_short, cot_float)
    key_grad = jnp.einsum('gqk,qgd->kd', score_short, query_float) * scaling
    query_grad = jnp.einsum('gqk,kd->qgd', score_short, key_float) * scaling
    return query_grad.astype(jnp.bfloat16), key_grad, value_grad


def reference(inputs, key_weight, value_weight, queries, output_cotangent, documents):
    keys = jnp.dot(inputs, key_weight, preferred_element_type=jnp.float32).astype(jnp.bfloat16)
    values = jnp.dot(inputs, value_weight, preferred_element_type=jnp.float32).astype(jnp.bfloat16)
    positions = jnp.arange(SEQ, dtype=jnp.int32)
    allowed = (documents[:, None] == documents[None, :]) & (positions[None, :] <= positions[:, None])
    row_width = GROUP * HD
    anchor = jnp.zeros((), jnp.int32)

    def per_head(flat_index):
        layer_index = (flat_index // KVH).astype(jnp.int32)
        head_index = (flat_index % KVH).astype(jnp.int32)
        column = (head_index * row_width).astype(jnp.int32)
        query = lax.dynamic_slice(queries, (layer_index, anchor, column), (1, SEQ, row_width))[0]
        cotangent = lax.dynamic_slice(output_cotangent, (layer_index, anchor, column), (1, SEQ, row_width))[0]
        key_column = (head_index * HD).astype(jnp.int32)
        key_tile = lax.dynamic_slice(keys, (anchor, key_column), (SEQ, HD))
        value_tile = lax.dynamic_slice(values, (anchor, key_column), (SEQ, HD))
        query_grad, key_grad, value_grad = backward_one(query.reshape(SEQ, GROUP, HD), key_tile, value_tile, cotangent.reshape(SEQ, GROUP, HD), allowed)
        return query_grad.reshape(SEQ, row_width), key_grad, value_grad

    query_grad, key_grad, value_grad = lax.map(per_head, jnp.arange(LAYERS * KVH, dtype=jnp.int32))
    query_gradient = query_grad.reshape(LAYERS, KVH, SEQ, row_width).transpose(0, 2, 1, 3).reshape(LAYERS, SEQ, KVH * row_width)
    key_total = jnp.sum(key_grad.reshape(LAYERS, KVH, SEQ, HD), axis=0).transpose(1, 0, 2).reshape(SEQ, KVH * HD)
    value_total = jnp.sum(value_grad.reshape(LAYERS, KVH, SEQ, HD), axis=0).transpose(1, 0, 2).reshape(SEQ, KVH * HD)
    key_short = key_total.astype(jnp.bfloat16)
    value_short = value_total.astype(jnp.bfloat16)
    contract = (((1,), (1,)), ((), ()))
    summed = lax.dot_general(key_short, key_weight, contract, preferred_element_type=jnp.float32)
    summed = summed + lax.dot_general(value_short, value_weight, contract, preferred_element_type=jnp.float32)
    return query_gradient, summed.astype(jnp.bfloat16)
```

```python
import functools

import jax
import jax.numpy as jnp
from jax import lax
from jax.experimental import pallas as pl
from jax.experimental.pallas import tpu as pltpu
from jax.sharding import PartitionSpec as P

MESH = pl.DeviceIdType.MESH
NT = (((1,), (1,)), ((), ()))
TN = (((0,), (0,)), ((), ()))
F32 = jnp.float32
BF16 = jnp.bfloat16


def backward_kernel(
    sizes,
    x_hbm,
    wk_hbm,
    wv_hbm,
    q_hbm,
    g_hbm,
    docs_hbm,
    qg_ref,
    ig_ref,
    x_v,
    w_v,
    qf,
    gf,
    kv,
    kvf,
    st,
    dpt,
    ds16,
    sbuf,
    rbuf,
    zsend,
    zrecv,
    far_w,
    far_kv,
    own_kv,
    own_v,
    docs_ref,
    load_sem,
    ag_send,
    ag_recv,
    rs_send,
    rs_recv,
    z_send,
    z_recv,
    far_send,
    far_recv,
):
    L, H, Q, r, R, S, D, hd, G, chunks, kb, line = sizes
    n = L * Q
    scaling = hd ** (-0.5)
    span = S // 2
    ly = lax.axis_index("layer")
    hh = lax.axis_index("head")
    qb = lax.axis_index("qblk")
    me = ly * Q + qb

    def needed(owner, block):
        above = owner * r < (block + 1) * R
        below = (owner + 1) * r - 1 >= block * R - span + 1
        return jnp.logical_and(above, below)

    def place(peer):
        return (peer // Q, hh, lax.rem(peer, Q))

    if L == 4 and Q == 2:
        row, col = ly // 2, lax.rem(ly, 2)
        far_layer = (1 - row) * 2 + 1 - col
        next_layers = [row * 2 + 1 - col, (1 - row) * 2 + col]
        peers = [far_layer * Q + qb, far_layer * Q + 1 - qb]
        peers += [layer * Q + qb for layer in next_layers]
        peers += [layer * Q + 1 - qb for layer in next_layers]
        peers += [ly * Q + 1 - qb]
    else:
        peers = [lax.rem(me + o, n) for o in range(1, n)]
    heads = [lax.rem(hh + o, H) for o in range(1, H)]

    barrier = pltpu.get_barrier_semaphore()
    for other in heads:
        pl.semaphore_signal(barrier, inc=1, device_id=(ly, other, qb), device_id_type=MESH)
    for peer in peers:
        pl.semaphore_signal(barrier, inc=1, device_id=place(peer), device_id_type=MESH)

    step = D // chunks
    loads = [pltpu.make_async_copy(x_hbm, x_v, load_sem.at[0])]
    for c in range(chunks):
        rows = pl.ds(c * step, step)
        loads.append(
            pltpu.make_async_copy(
                wk_hbm.at[rows, :], w_v.at[rows, pl.ds(0, hd)], load_sem.at[1 + 2 * c]
            )
        )
        loads.append(
            pltpu.make_async_copy(
                wv_hbm.at[rows, :], w_v.at[rows, pl.ds(hd, hd)], load_sem.at[2 + 2 * c]
            )
        )
    base = 1 + 2 * chunks
    docs_load = pltpu.make_async_copy(docs_hbm, docs_ref, load_sem.at[base + 2 * G])
    docs_load.start()
    for g in range(G):
        cols = pl.ds(g * hd, hd)
        rows = pl.ds(g * R, R)
        loads.append(
            pltpu.make_async_copy(q_hbm.at[0, :, cols], qf.at[rows, :], load_sem.at[base + 2 * g])
        )
        loads.append(
            pltpu.make_async_copy(
                g_hbm.at[0, :, cols], gf.at[rows, :], load_sem.at[base + 2 * g + 1]
            )
        )
    for load in loads:
        load.start()

    loads[0].wait()
    acc = jnp.zeros((r, 2 * hd), F32)
    for c in range(chunks):
        loads[1 + 2 * c].wait()
        loads[2 + 2 * c].wait()
        acc = acc + jnp.dot(
            x_v[:, c * step : (c + 1) * step],
            w_v[c * step : (c + 1) * step, :],
            preferred_element_type=F32,
        )
    mine = acc.astype(BF16)
    for k in range(2):
        own_v[k] = mine[:, k * hd : (k + 1) * hd]
    pl.semaphore_wait(barrier, n - 1 + H - 1)

    def gather_copy(k, peer, slot):
        return pltpu.make_async_remote_copy(
            src_ref=own_v.at[k],
            dst_ref=kv.at[k, slot],
            send_sem=ag_send.at[k * n + peer],
            recv_sem=ag_recv.at[k * n + slot],
            device_id=place(peer),
            device_id_type=MESH,
        )

    for k in range(2):
        for peer in peers:

            @pl.when(needed(me, lax.rem(peer, Q)))
            def _(k=k, peer=peer):
                gather_copy(k, peer, me).start()

    width = D // H
    if line:
        half = width // Q
        wide = 256
        pieces = width // wide
        at_edge = jnp.logical_or(hh == 0, hh == 3)
        edge = jnp.where(hh < 2, 0, 3)
        near_mid = jnp.where(hh < 2, 1, 2)
        partner = jnp.where(at_edge, near_mid, edge)
        far = 3 - hh
        far_copies = []
        for i, w_hbm in enumerate((wk_hbm, wv_hbm)):
            far_copies.append(
                pltpu.make_async_remote_copy(
                    src_ref=w_hbm.at[
                        pl.ds(pl.multiple_of(far * width + qb * half, half), half), :
                    ],
                    dst_ref=far_w.at[
                        pl.ds(pl.multiple_of(qb * half, half), half), pl.ds(i * hd, hd)
                    ],
                    send_sem=far_send.at[i],
                    recv_sem=far_recv.at[i],
                    device_id=(ly, far, qb),
                    device_id_type=MESH,
                )
            )

        @pl.when(at_edge)
        def _():
            for copy in far_copies:
                copy.start()

    @pl.when(needed(me, qb))
    def _():
        for k in range(2):
            kv[k, me] = mine[:, k * hd : (k + 1) * hd]

    blank = jnp.zeros((r, hd), BF16)
    for d in range(n):

        @pl.when(jnp.logical_not(needed(d, qb)))
        def _(d=d):
            kv[0, d] = blank
            kv[1, d] = blank

        @pl.when(jnp.logical_not(needed(me, d % Q)))
        def _(d=d):
            rbuf[0, d] = blank
            rbuf[1, d] = blank

    docs_load.wait()
    docs = docs_ref[...].reshape(1, S)
    own_docs = docs[:, 0:R]
    for b in range(1, Q):
        own_docs = jnp.where(qb == b, docs[:, b * R : (b + 1) * R], own_docs)
    own_docs = jnp.concatenate([own_docs] * G, axis=1)
    key_docs = jnp.transpose(jnp.broadcast_to(docs, (128, S)))[:, 0:1]
    first_key = jnp.sum((key_docs < own_docs).astype(F32), axis=0, keepdims=True).astype(jnp.int32)
    position = qb * R + jnp.concatenate(
        [lax.broadcasted_iota(jnp.int32, (1, R), 1)] * G, axis=1
    )


    for load in loads[base:]:
        load.wait()

    def gathered(k):
        for peer in peers:

            @pl.when(needed(peer, qb))
            def _(peer=peer):
                gather_copy(k, peer, peer).wait_recv()

        if r % 16 == 0:
            kvf[k] = kv[k].reshape(S, hd)
        else:
            for d in range(n):
                kvf[k, d * r : (d + 1) * r, :] = kv[k, d]

    gathered(0)

    cols = G * R
    blocks = S // kb

    def run(body, carry):
        if blocks == 1:
            return body(0, carry)
        return lax.fori_loop(0, blocks, body, carry)

    def rows_of(j):
        return pl.ds(pl.multiple_of(j * kb, kb), kb) if blocks > 1 else pl.ds(0, kb)

    def scores(j, top):
        rows = rows_of(j)
        key_pos = j * kb + lax.broadcasted_iota(jnp.int32, (kb, cols), 0)
        visible = (key_pos >= first_key) & (key_pos <= position)
        s = lax.dot_general(kvf[0, rows, :], qf[...], NT, preferred_element_type=F32) * scaling
        s = jnp.where(visible, s, -1e30)
        st[rows, :] = s
        return jnp.maximum(top, jnp.max(s, axis=0, keepdims=True))

    top = run(scores, jnp.full((1, cols), -1e30, F32))

    def totals(j, total):
        rows = rows_of(j)
        p = jnp.exp(st[rows, :] - top)
        st[rows, :] = p
        return total + jnp.sum(p, axis=0, keepdims=True)

    zero_row = jnp.zeros((1, cols), F32)
    inverse = 1.0 / run(totals, zero_row)

    def keep(k, j, grad):
        grad = grad.astype(BF16)
        if blocks == 1:
            sbuf[k] = grad.reshape(n, r, hd)
        else:
            per = kb // r
            for i in range(per):
                sbuf[k, j * per + i] = grad[i * r : (i + 1) * r]

    def value_grads(j, carry):
        rows = rows_of(j)
        p = st[rows, :] * inverse
        st[rows, :] = p
        keep(1, j, jnp.dot(p.astype(BF16), gf[...], preferred_element_type=F32))
        return carry

    def reduce_copy(k, peer, slot):
        return pltpu.make_async_remote_copy(
            src_ref=sbuf.at[k, peer],
            dst_ref=rbuf.at[k, slot],
            send_sem=rs_send.at[k * n + peer],
            recv_sem=rs_recv.at[k * n + slot],
            device_id=place(peer),
            device_id_type=MESH,
        )

    def scatter(k):
        for peer in peers:

            @pl.when(needed(peer, qb))
            def _(peer=peer):
                reduce_copy(k, peer, me).start()

        @pl.when(needed(me, qb))
        def _():
            rbuf[k, me] = sbuf[k, me]

    run(value_grads, 0)
    scatter(1)
    gathered(1)

    def dots(j, dot):
        rows = rows_of(j)
        grad = lax.dot_general(kvf[1, rows, :], gf[...], NT, preferred_element_type=F32)
        dpt[rows, :] = grad
        return dot + jnp.sum(st[rows, :] * grad, axis=0, keepdims=True)

    delta = run(dots, zero_row)

    def key_grads(j, carry):
        rows = rows_of(j)
        ds = (st[rows, :] * (dpt[rows, :] - delta)).astype(BF16)
        ds16[rows, :] = ds
        keep(0, j, jnp.dot(ds, qf[...], preferred_element_type=F32) * scaling)
        return carry

    run(key_grads, 0)
    scatter(0)

    def query_grads(j, carry):
        rows = rows_of(j)
        return carry + lax.dot_general(
            ds16[rows, :], kvf[0, rows, :], TN, preferred_element_type=F32
        )

    dq = run(query_grads, jnp.zeros((cols, hd), F32)) * scaling
    for g in range(G):
        qg_ref[0, :, g * hd : (g + 1) * hd] = dq[g * R : (g + 1) * R].astype(BF16)

    for k in (1, 0):
        for peer in peers:

            @pl.when(needed(me, lax.rem(peer, Q)))
            def _(k=k, peer=peer):
                reduce_copy(k, peer, peer).wait_recv()

    halves = []
    for k in range(2):
        owned = rbuf[k, 0].astype(F32)
        for d in range(1, n):
            owned = owned + rbuf[k, d].astype(F32)
        halves.append(owned.astype(BF16))
    owned = jnp.concatenate(halves, axis=1)

    def part_of(head):
        rows = pl.ds(pl.multiple_of(head * width, width), width)
        return lax.dot_general(owned, w_v[rows, :], NT, preferred_element_type=F32)

    if line:
        own_kv[...] = owned

        def chunk_of(head, c):
            rows = pl.ds(pl.multiple_of(head * width + c * wide, wide), wide)
            return lax.dot_general(owned, w_v[rows, :], NT, preferred_element_type=F32)

        def stream(k, c, head):
            return pltpu.make_async_remote_copy(
                src_ref=zsend.at[k, c],
                dst_ref=zrecv.at[k, c],
                send_sem=z_send.at[k * pieces + c],
                recv_sem=z_recv.at[k * pieces + c],
                device_id=(ly, head, qb),
                device_id_type=MESH,
            )

        factor = pltpu.make_async_remote_copy(
            src_ref=own_kv,
            dst_ref=far_kv,
            send_sem=far_send.at[2],
            recv_sem=far_recv.at[2],
            device_id=(ly, far, qb),
            device_id_type=MESH,
        )
        first_head = jnp.where(at_edge, 3 - near_mid, edge)
        second_head = jnp.where(at_edge, near_mid, 3 - edge)

        @pl.when(at_edge)
        def _():
            factor.start()

        for c in range(pieces):
            zsend[0, c] = chunk_of(first_head, c).astype(BF16)
            stream(0, c, partner).start()
        for c in range(pieces):
            zsend[1, c] = chunk_of(second_head, c).astype(BF16)
            stream(1, c, second_head).start()

        @pl.when(jnp.logical_not(at_edge))
        def _():
            for c in range(pieces):
                mine2 = chunk_of(3 - hh, c)
                stream(0, c, partner).wait_recv()
                zsend[2, c] = (mine2 + zrecv[0, c].astype(F32)).astype(BF16)
                stream(2, c, 3 - hh).start()
            for c in range(pieces):
                total_c = chunk_of(hh, c)
                stream(1, c, second_head).wait_recv()
                total_c = total_c + zrecv[1, c].astype(F32)
                stream(2, c, 3 - hh).wait_recv()
                total_c = total_c + zrecv[2, c].astype(F32)
                ig_ref[:, c * wide : (c + 1) * wide] = total_c.astype(BF16)
            for c in range(pieces):
                stream(2, c, 3 - hh).wait_send()

        @pl.when(at_edge)
        def _():
            for copy in far_copies:
                copy.wait_recv()
            share = pl.ds(pl.multiple_of(qb * half, half), half)
            swap = pltpu.make_async_remote_copy(
                src_ref=far_w.at[share, :],
                dst_ref=far_w.at[share, :],
                send_sem=far_send.at[3],
                recv_sem=far_recv.at[3],
                device_id=(ly, hh, 1 - qb),
                device_id_type=MESH,
            )
            swap.start()
            other_share = pl.ds(pl.multiple_of((1 - qb) * half, half), half)
            arriving = pltpu.make_async_remote_copy(
                src_ref=far_w.at[share, :],
                dst_ref=far_w.at[other_share, :],
                send_sem=far_send.at[3],
                recv_sem=far_recv.at[3],
                device_id=(ly, hh, 1 - qb),
                device_id_type=MESH,
            )
            factor.wait_recv()
            arriving.wait_recv()
            for c in range(pieces):
                total_c = chunk_of(hh, c) + lax.dot_general(
                    far_kv[...],
                    far_w[c * wide : (c + 1) * wide, :],
                    NT,
                    preferred_element_type=F32,
                )
                stream(0, c, partner).wait_recv()
                total_c = total_c + zrecv[0, c].astype(F32)
                stream(1, c, second_head).wait_recv()
                total_c = total_c + zrecv[1, c].astype(F32)
                ig_ref[:, c * wide : (c + 1) * wide] = total_c.astype(BF16)
            for copy in far_copies:
                copy.wait_send()
            factor.wait_send()
            swap.wait_send()

        for c in range(pieces):
            stream(0, c, partner).wait_send()
            stream(1, c, second_head).wait_send()
    else:
        z_copies = []
        for o in range(1, H):
            other = heads[o - 1]
            zsend[o - 1] = part_of(other).astype(BF16)
            copy = pltpu.make_async_remote_copy(
                src_ref=zsend.at[o - 1],
                dst_ref=zrecv.at[o - 1],
                send_sem=z_send.at[o - 1],
                recv_sem=z_recv.at[o - 1],
                device_id=(ly, other, qb),
                device_id_type=MESH,
            )
            copy.start()
            z_copies.append(copy)
        result = part_of(hh)
        for o, copy in enumerate(z_copies):
            copy.wait_recv()
            result = result + zrecv[o].astype(F32)
        ig_ref[...] = result.astype(BF16)

        for copy in z_copies:
            copy.wait_send()

    for k in range(2):
        for peer in peers:

            @pl.when(needed(me, lax.rem(peer, Q)))
            def _(k=k, peer=peer):
                gather_copy(k, peer, me).wait_send()

            @pl.when(needed(peer, qb))
            def _(k=k, peer=peer):
                reduce_copy(k, peer, me).wait_send()


def scoped_kernel(sizes, *refs):
    L, H, Q, r, R, S, D, hd, G, chunks, kb, line = sizes
    n = L * Q
    sends = 3 * (D // H // 256) if line else H - 1
    dma = pltpu.SemaphoreType.DMA
    counts = [2 + 2 * chunks + 2 * G, 2 * n, 2 * n, 2 * n, 2 * n, sends, sends, 4, 4]
    pl.run_scoped(lambda *sems: backward_kernel(sizes, *refs, *sems), *[dma((c,)) for c in counts])


def write_kernel(qg_in, ig_in, qg_out, ig_out, sems):
    copies = [
        pltpu.make_async_copy(qg_in, qg_out, sems.at[0]),
        pltpu.make_async_copy(ig_in, ig_out, sems.at[1]),
    ]
    for copy in copies:
        copy.start()
    for copy in copies:
        copy.wait()


def solution(mesh):
    L, H, Q = mesh.shape["layer"], mesh.shape["head"], mesh.shape["qblk"]
    n = L * Q

    def local(inputs, key_weight, value_weight, queries, output_cotangent, documents):
        r, D = inputs.shape
        hd = key_weight.shape[1]
        _, R, wide = queries.shape
        G = wide // hd
        S = documents.shape[0]
        chunks = 4
        kb = min(S, 384)
        line = H == 4 and Q == 2 and (D // H) % 256 == 0
        sizes = (L, H, Q, r, R, S, D, hd, G, chunks, kb, line)
        width = D // H
        streams = (3, width // 256, r, 256) if line else (H - 1, r, width)
        far_rows = width if line else 16
        cols = G * R
        anywhere = pl.BlockSpec(memory_space=pl.ANY)
        vmem = pl.BlockSpec(memory_space=pltpu.VMEM)
        dma = pltpu.SemaphoreType.DMA
        query_grad, input_grad = pl.pallas_call(
            functools.partial(scoped_kernel, sizes),
            out_shape=(
                pltpu.VMEM(queries.shape, BF16),
                pltpu.VMEM((r, D // H), BF16),
            ),
            in_specs=[anywhere] * 6,
            out_specs=(vmem, vmem),
            scratch_shapes=[
                pltpu.VMEM((r, D), BF16),
                pltpu.VMEM((D, 2 * hd), BF16),
                pltpu.VMEM((cols, hd), BF16),
                pltpu.VMEM((cols, hd), BF16),
                pltpu.VMEM((2, n, r, hd), BF16),
                pltpu.VMEM((2, S, hd), BF16),
                pltpu.VMEM((S, cols), F32),
                pltpu.VMEM((S, cols), F32),
                pltpu.VMEM((S, cols), BF16),
                pltpu.VMEM((2, n, r, hd), BF16),
                pltpu.VMEM((2, n, r, hd), BF16),
                pltpu.VMEM(streams, BF16),
                pltpu.VMEM(streams, BF16),
                pltpu.VMEM((far_rows, 2 * hd), BF16),
                pltpu.VMEM((r, 2 * hd), BF16),
                pltpu.VMEM((r, 2 * hd), BF16),
                pltpu.VMEM((2, r, hd), BF16),
                pltpu.VMEM((S,), jnp.int32),
            ],
            compiler_params=pltpu.CompilerParams(
                collective_id=0, has_side_effects=True, vmem_limit_bytes=60 * 1024 * 1024
            ),
        )(
            inputs,
            key_weight,
            value_weight,
            queries,
            output_cotangent,
            documents,
        )
        return pl.pallas_call(
            write_kernel,
            out_shape=(
                jax.ShapeDtypeStruct(query_grad.shape, BF16),
                jax.ShapeDtypeStruct(input_grad.shape, BF16),
            ),
            in_specs=[vmem] * 2,
            out_specs=(anywhere, anywhere),
            scratch_shapes=[dma((2,))],
            compiler_params=pltpu.CompilerParams(vmem_limit_bytes=1024 * 1024),
        )(query_grad, input_grad)

    placed = (
        P(("layer", "qblk"), None),
        P(None, "head"),
        P(None, "head"),
        P("layer", "qblk", "head"),
        P("layer", "qblk", "head"),
        P(),
    )
    return jax.shard_map(
        local,
        mesh=mesh,
        in_specs=placed,
        out_specs=(P("layer", "qblk", "head"), P(("layer", "qblk"), "head")),
        check_vma=False,
    )
```

```python
import functools

import jax
import jax.numpy as jnp
from jax import lax
from jax.experimental import pallas as pl
from jax.experimental.pallas import tpu as pltpu
from jax.sharding import PartitionSpec as P

MESH = pl.DeviceIdType.MESH
NT = (((1,), (1,)), ((), ()))
TN = (((0,), (0,)), ((), ()))
F32 = jnp.float32
BF16 = jnp.bfloat16


def backward_kernel(
    sizes,
    x_hbm,
    wk_hbm,
    wv_hbm,
    q_hbm,
    g_hbm,
    docs_hbm,
    qg_ref,
    ig_ref,
    x_v,
    w_v,
    qf,
    gf,
    kv,
    kvf,
    st,
    dpt,
    ds16,
    acc_kv,
    sbuf,
    rbuf,
    zsend,
    zrecv,
    far_w,
    far_kv,
    own_kv,
    total,
    own_v,
    docs_ref,
    load_sem,
    ag_send,
    ag_recv,
    rs_send,
    rs_recv,
    z_send,
    z_recv,
    wz_send,
    wz_recv,
    wx_send,
    wx_recv,
    wt_send,
    wt_recv,
    kv_send,
    kv_recv,
):
    L, H, Q, r, R, S, D, hd, G, chunks, kb, line, band = sizes
    n = L * Q
    scaling = hd ** (-0.5)
    span = S // 2
    ly = lax.axis_index("layer")
    hh = lax.axis_index("head")
    qb = lax.axis_index("qblk")
    me = ly * Q + qb

    def needed(owner, block):
        above = owner * r < (block + 1) * R
        below = (owner + 1) * r - 1 >= block * R - span + 1
        return jnp.logical_and(above, below)

    def place(peer):
        return (peer // Q, hh, lax.rem(peer, Q))

    if L == 4 and Q == 2:
        row, col = ly // 2, lax.rem(ly, 2)
        far_layer = (1 - row) * 2 + 1 - col
        next_layers = [row * 2 + 1 - col, (1 - row) * 2 + col]
        peers = [far_layer * Q + qb, far_layer * Q + 1 - qb]
        peers += [layer * Q + qb for layer in next_layers]
        peers += [layer * Q + 1 - qb for layer in next_layers]
        peers += [ly * Q + 1 - qb]
    else:
        peers = [lax.rem(me + o, n) for o in range(1, n)]
    heads = [lax.rem(hh + o, H) for o in range(1, H)]

    barrier = pltpu.get_barrier_semaphore()
    for other in heads:
        pl.semaphore_signal(barrier, inc=1, device_id=(ly, other, qb), device_id_type=MESH)
    for peer in peers:
        pl.semaphore_signal(barrier, inc=1, device_id=place(peer), device_id_type=MESH)

    step = D // chunks
    loads = []
    for c in range(chunks):
        rows = pl.ds(c * step, step)
        loads.append(
            pltpu.make_async_copy(x_hbm.at[:, rows], x_v.at[:, rows], load_sem.at[3 * c])
        )
        loads.append(
            pltpu.make_async_copy(
                wk_hbm.at[rows, :], w_v.at[rows, pl.ds(0, hd)], load_sem.at[3 * c + 1]
            )
        )
        loads.append(
            pltpu.make_async_copy(
                wv_hbm.at[rows, :], w_v.at[rows, pl.ds(hd, hd)], load_sem.at[3 * c + 2]
            )
        )
    base = 3 * chunks
    docs_load = pltpu.make_async_copy(docs_hbm, docs_ref, load_sem.at[base + 2])
    docs_load.start()
    parts = R // band if band else 1
    tall = R // parts
    for i in range(parts):
        for g in range(G):
            cols = pl.ds(g * hd, hd)
            take = pl.ds(i * tall, tall)
            rows = pl.ds((i * G + g) * tall, tall)
            loads.append(
                pltpu.make_async_copy(q_hbm.at[0, take, cols], qf.at[rows, :], load_sem.at[base])
            )
            loads.append(
                pltpu.make_async_copy(
                    g_hbm.at[0, take, cols], gf.at[rows, :], load_sem.at[base + 1]
                )
            )
    for load in loads:
        load.start()

    acc = jnp.zeros((r, 2 * hd), F32)
    for c in range(chunks):
        for load in loads[3 * c : 3 * c + 3]:
            load.wait()
        acc = acc + jnp.dot(
            x_v[:, c * step : (c + 1) * step],
            w_v[c * step : (c + 1) * step, :],
            preferred_element_type=F32,
        )
    mine = acc.astype(BF16)
    for k in range(2):
        own_v[k] = mine[:, k * hd : (k + 1) * hd]
    pl.semaphore_wait(barrier, n - 1 + H - 1)

    def gather_copy(k, peer, slot):
        return pltpu.make_async_remote_copy(
            src_ref=own_v.at[k],
            dst_ref=kv.at[k, slot],
            send_sem=ag_send.at[k * n + peer],
            recv_sem=ag_recv.at[k * n + slot],
            device_id=place(peer),
            device_id_type=MESH,
        )

    for k in range(2):
        for peer in peers:

            @pl.when(needed(me, lax.rem(peer, Q)))
            def _(k=k, peer=peer):
                gather_copy(k, peer, me).start()

    width = D // H
    if line:
        half = width // Q
        piece = half // L
        wide = 256
        pieces = width // wide
        at_edge = jnp.logical_or(hh == 0, hh == 3)
        near = hh + 1 - 2 * lax.rem(hh, 2)
        second = lax.rem(hh + 2, 4)
        opposite = 3 - hh
        qb_rows = pl.ds(pl.multiple_of(qb * half, half), half)
        other_rows = pl.ds(pl.multiple_of((1 - qb) * half, half), half)

        column = lax.rem(ly, 2)
        spots = [ly, column, 2 + ly // 2]
        beside = [ly + 1 - 2 * column, lax.rem(ly + 2, L)]

        def piece_rows(first, spot):
            return pl.ds(pl.multiple_of(first + qb * half + spot * piece, piece), piece)

        def prefetch(way, head):
            return pltpu.make_async_remote_copy(
                src_ref=w_v.at[piece_rows(head * width, spots[way]), :],
                dst_ref=far_w.at[min(way, 1), piece_rows(0, spots[way]), :],
                send_sem=wz_send.at[way],
                recv_sem=wz_recv.at[way],
                device_id=(ly, head, qb),
                device_id_type=MESH,
            )

        def share(layer, source):
            return pltpu.make_async_remote_copy(
                src_ref=far_w.at[0, piece_rows(0, source), :],
                dst_ref=far_w.at[0, piece_rows(0, source), :],
                send_sem=wx_send.at[layer],
                recv_sem=wx_recv.at[source],
                device_id=(layer, hh, qb),
                device_id_type=MESH,
            )

        def swap(way, spot):
            return pltpu.make_async_remote_copy(
                src_ref=far_w.at[1, piece_rows(0, spot), :],
                dst_ref=far_w.at[1, piece_rows(0, spot), :],
                send_sem=wx_send.at[L + way],
                recv_sem=wx_recv.at[L + way],
                device_id=(beside[way], hh, qb),
                device_id_type=MESH,
            )

        def twin(slot, rows):
            return pltpu.make_async_remote_copy(
                src_ref=far_w.at[slot, rows, :],
                dst_ref=far_w.at[slot, rows, :],
                send_sem=wt_send.at[slot],
                recv_sem=wt_recv.at[slot],
                device_id=(ly, hh, 1 - qb),
                device_id_type=MESH,
            )

        other_layers = [lax.rem(ly + o, L) for o in range(1, L)]

        prefetch(0, second).start()

    @pl.when(needed(me, qb))
    def _():
        for k in range(2):
            kv[k, me] = mine[:, k * hd : (k + 1) * hd]

    blank = jnp.zeros((r, hd), BF16)
    for d in range(n):

        @pl.when(jnp.logical_not(needed(d, qb)))
        def _(d=d):
            kv[0, d] = blank
            kv[1, d] = blank

        @pl.when(jnp.logical_not(needed(me, d % Q)))
        def _(d=d):
            rbuf[0, d] = blank
            rbuf[1, d] = blank

    docs_load.wait()
    docs = docs_ref[...].reshape(1, S)
    own_docs = docs[:, 0:R]
    for b in range(1, Q):
        own_docs = jnp.where(qb == b, docs[:, b * R : (b + 1) * R], own_docs)
    key_docs = jnp.transpose(jnp.broadcast_to(docs, (128, S)))[:, 0:1]
    first_key = jnp.sum((key_docs < own_docs).astype(F32), axis=0, keepdims=True).astype(jnp.int32)
    position = qb * R + lax.broadcasted_iota(jnp.int32, (1, R), 1)
    if band:
        first_keys = []
        positions = []
        for i in range(parts):
            take = slice(i * tall, (i + 1) * tall)
            first_keys.append(jnp.concatenate([first_key[:, take]] * G, axis=1))
            positions.append(jnp.concatenate([position[:, take]] * G, axis=1))
    else:
        first_key = jnp.concatenate([first_key] * G, axis=1)
        position = jnp.concatenate([position] * G, axis=1)

    pltpu.make_async_copy(qf, qf, load_sem.at[base]).wait()
    pltpu.make_async_copy(gf, gf, load_sem.at[base + 1]).wait()

    def gathered(k):
        for peer in peers:

            @pl.when(needed(peer, qb))
            def _(peer=peer):
                gather_copy(k, peer, peer).wait_recv()

        if r % 16 == 0:
            kvf[k] = kv[k].reshape(S, hd)
        else:
            for d in range(n):
                kvf[k, d * r : (d + 1) * r, :] = kv[k, d]

    gathered(0)
    if line:

        @pl.when(at_edge)
        def _():
            prefetch(1, opposite).start()
            prefetch(2, opposite).start()


    def reduce_copy(k, peer, slot):
        return pltpu.make_async_remote_copy(
            src_ref=sbuf.at[k, peer],
            dst_ref=rbuf.at[k, slot],
            send_sem=rs_send.at[k * n + peer],
            recv_sem=rs_recv.at[k * n + slot],
            device_id=place(peer),
            device_id_type=MESH,
        )

    def scatter(k):
        for peer in peers:

            @pl.when(needed(peer, qb))
            def _(peer=peer):
                reduce_copy(k, peer, me).start()

        @pl.when(needed(me, qb))
        def _():
            rbuf[k, me] = sbuf[k, me]

    if band:
        high = span + tall
        wide_cols = G * tall
        starts = [
            pl.multiple_of(jnp.maximum(qb * R + i * tall - span, 0), tall) for i in range(parts)
        ]
        windows = [pl.ds(start, high) for start in starts]
        takes = [slice(i * wide_cols, (i + 1) * wide_cols) for i in range(parts)]

        def hand_over(k, factor):
            for d in range(n):
                grad = acc_kv[k, d * r : (d + 1) * r, :]
                sbuf[k, d] = (grad * factor if factor else grad).astype(BF16)

        acc_kv[...] = jnp.zeros(acc_kv.shape, F32)
        tops = []
        for i in range(parts):
            key_pos = starts[i] + lax.broadcasted_iota(jnp.int32, (high, wide_cols), 0)
            visible = (key_pos >= first_keys[i]) & (key_pos <= positions[i])
            s = lax.dot_general(
                kvf[0, windows[i], :], qf[takes[i], :], NT, preferred_element_type=F32
            )
            s = jnp.where(visible, s * scaling, -1e30)
            st[i] = s
            tops.append(jnp.max(s, axis=0, keepdims=True))
        for i in range(parts):
            p = jnp.exp(st[i] - tops[i])
            p = p * (1.0 / jnp.sum(p, axis=0, keepdims=True))
            st[i] = p
            acc_kv[1, windows[i], :] += jnp.dot(
                p.astype(BF16), gf[takes[i], :], preferred_element_type=F32
            )
        hand_over(1, None)
        scatter(1)
        gathered(1)
        for i in range(parts):
            grad = lax.dot_general(
                kvf[1, windows[i], :], gf[takes[i], :], NT, preferred_element_type=F32
            )
            p = st[i]
            delta = jnp.sum(p * grad, axis=0, keepdims=True)
            ds = (p * (grad - delta)).astype(BF16)
            ds16[i] = ds
            acc_kv[0, windows[i], :] += jnp.dot(ds, qf[takes[i], :], preferred_element_type=F32)
        hand_over(0, scaling)
        scatter(0)
        for i in range(parts):
            dq = scaling * lax.dot_general(
                ds16[i], kvf[0, windows[i], :], TN, preferred_element_type=F32
            )
            for g in range(G):
                qg_ref[0, i * tall : (i + 1) * tall, g * hd : (g + 1) * hd] = dq[
                    g * tall : (g + 1) * tall
                ].astype(BF16)
    else:
        cols = G * R
        blocks = S // kb

        def run(body, carry):
            if blocks == 1:
                return body(0, carry)
            return lax.fori_loop(0, blocks, body, carry)

        def rows_of(j):
            return pl.ds(pl.multiple_of(j * kb, kb), kb) if blocks > 1 else pl.ds(0, kb)

        def scores(j, top):
            rows = rows_of(j)
            key_pos = j * kb + lax.broadcasted_iota(jnp.int32, (kb, cols), 0)
            visible = (key_pos >= first_key) & (key_pos <= position)
            s = lax.dot_general(kvf[0, rows, :], qf[...], NT, preferred_element_type=F32) * scaling
            s = jnp.where(visible, s, -1e30)
            st[rows, :] = s
            return jnp.maximum(top, jnp.max(s, axis=0, keepdims=True))

        top = run(scores, jnp.full((1, cols), -1e30, F32))

        def totals(j, total):
            rows = rows_of(j)
            p = jnp.exp(st[rows, :] - top)
            st[rows, :] = p
            return total + jnp.sum(p, axis=0, keepdims=True)

        zero_row = jnp.zeros((1, cols), F32)
        inverse = 1.0 / run(totals, zero_row)

        def keep(k, j, grad):
            grad = grad.astype(BF16)
            if blocks == 1:
                sbuf[k] = grad.reshape(n, r, hd)
            else:
                per = kb // r
                for i in range(per):
                    sbuf[k, j * per + i] = grad[i * r : (i + 1) * r]

        def value_grads(j, carry):
            rows = rows_of(j)
            p = st[rows, :] * inverse
            st[rows, :] = p
            keep(1, j, jnp.dot(p.astype(BF16), gf[...], preferred_element_type=F32))
            return carry

        run(value_grads, 0)
        scatter(1)
        gathered(1)

        def dots(j, dot):
            rows = rows_of(j)
            grad = lax.dot_general(kvf[1, rows, :], gf[...], NT, preferred_element_type=F32)
            dpt[rows, :] = grad
            return dot + jnp.sum(st[rows, :] * grad, axis=0, keepdims=True)

        delta = run(dots, zero_row)

        def key_grads(j, carry):
            rows = rows_of(j)
            ds = (st[rows, :] * (dpt[rows, :] - delta)).astype(BF16)
            ds16[rows, :] = ds
            keep(0, j, jnp.dot(ds, qf[...], preferred_element_type=F32) * scaling)
            return carry

        run(key_grads, 0)
        scatter(0)

        def query_grads(j, carry):
            rows = rows_of(j)
            return carry + lax.dot_general(
                ds16[rows, :], kvf[0, rows, :], TN, preferred_element_type=F32
            )

        dq = run(query_grads, jnp.zeros((cols, hd), F32)) * scaling
        for g in range(G):
            qg_ref[0, :, g * hd : (g + 1) * hd] = dq[g * R : (g + 1) * R].astype(BF16)

    if line:
        prefetch(0, second).wait_recv()
        for layer in other_layers:
            share(layer, ly).start()

    for k in (1, 0):
        for peer in peers:

            @pl.when(needed(me, lax.rem(peer, Q)))
            def _(k=k, peer=peer):
                reduce_copy(k, peer, peer).wait_recv()

    halves = []
    for k in range(2):
        owned = rbuf[k, 0].astype(F32)
        for d in range(1, n):
            owned = owned + rbuf[k, d].astype(F32)
        halves.append(owned.astype(BF16))
    owned = jnp.concatenate(halves, axis=1)

    def part_of(head):
        rows = pl.ds(pl.multiple_of(head * width, width), width)
        return lax.dot_general(owned, w_v[rows, :], NT, preferred_element_type=F32)

    if line:
        own_kv[...] = owned

        def chunk_of(head, c):
            rows = pl.ds(pl.multiple_of(head * width + c * wide, wide), wide)
            return lax.dot_general(owned, w_v[rows, :], NT, preferred_element_type=F32)

        def far_chunk(slot, c):
            return lax.dot_general(
                far_kv[slot],
                far_w[slot, c * wide : (c + 1) * wide, :],
                NT,
                preferred_element_type=F32,
            )

        def factor(slot, head):
            return pltpu.make_async_remote_copy(
                src_ref=own_kv,
                dst_ref=far_kv.at[slot],
                send_sem=kv_send.at[slot],
                recv_sem=kv_recv.at[slot],
                device_id=(ly, head, qb),
                device_id_type=MESH,
            )

        def stream(k, c, head):
            return pltpu.make_async_remote_copy(
                src_ref=zsend.at[k, c],
                dst_ref=zrecv.at[k, c],
                send_sem=z_send.at[k * pieces + c],
                recv_sem=z_recv.at[k * pieces + c],
                device_id=(ly, head, qb),
                device_id_type=MESH,
            )

        @pl.when(at_edge)
        def _():
            factor(1, opposite).start()

        factor(0, second).start()

        @pl.when(jnp.logical_not(at_edge))
        def _():
            for c in range(pieces):
                zsend[1, c] = chunk_of(opposite, c).astype(BF16)
                stream(1, c, opposite).start()

        for c in range(pieces):
            zsend[0, c] = chunk_of(near, c).astype(BF16)
            stream(0, c, near).start()

        for c in range(pieces):
            total[:, c * wide : (c + 1) * wide] = chunk_of(hh, c)

        @pl.when(at_edge)
        def _():
            for way in (1, 2):
                prefetch(way, opposite).wait_recv()
                swap(way - 1, spots[way]).start()

        for layer in other_layers:
            share(layer, layer).wait_recv()
        twin(0, qb_rows).start()

        @pl.when(at_edge)
        def _():
            swap(0, 1 - column).wait_recv()
            swap(1, 3 - ly // 2).wait_recv()
            twin(1, qb_rows).start()

        factor(0, second).wait_recv()
        twin(0, other_rows).wait_recv()
        for c in range(pieces):
            total[:, c * wide : (c + 1) * wide] += far_chunk(0, c)

        @pl.when(at_edge)
        def _():
            factor(1, opposite).wait_recv()
            twin(1, other_rows).wait_recv()
            for c in range(pieces):
                total[:, c * wide : (c + 1) * wide] += far_chunk(1, c)

        @pl.when(jnp.logical_not(at_edge))
        def _():
            for c in range(pieces):
                stream(1, c, opposite).wait_recv()
                total[:, c * wide : (c + 1) * wide] += zrecv[1, c].astype(F32)

        for c in range(pieces):
            stream(0, c, near).wait_recv()
            cols_c = slice(c * wide, (c + 1) * wide)
            ig_ref[:, cols_c] = (total[:, cols_c] + zrecv[0, c].astype(F32)).astype(BF16)

        @pl.when(at_edge)
        def _():
            for way in (1, 2):
                prefetch(way, opposite).wait_send()
                swap(way - 1, spots[way]).wait_send()
            twin(1, qb_rows).wait_send()
            factor(1, opposite).wait_send()

        @pl.when(jnp.logical_not(at_edge))
        def _():
            for c in range(pieces):
                stream(1, c, opposite).wait_send()

        prefetch(0, second).wait_send()
        for layer in other_layers:
            share(layer, ly).wait_send()
        twin(0, qb_rows).wait_send()
        factor(0, second).wait_send()
        for c in range(pieces):
            stream(0, c, near).wait_send()
    else:
        z_copies = []
        for o in range(1, H):
            other = heads[o - 1]
            zsend[o - 1] = part_of(other).astype(BF16)
            copy = pltpu.make_async_remote_copy(
                src_ref=zsend.at[o - 1],
                dst_ref=zrecv.at[o - 1],
                send_sem=z_send.at[o - 1],
                recv_sem=z_recv.at[o - 1],
                device_id=(ly, other, qb),
                device_id_type=MESH,
            )
            copy.start()
            z_copies.append(copy)
        result = part_of(hh)
        for o, copy in enumerate(z_copies):
            copy.wait_recv()
            result = result + zrecv[o].astype(F32)
        ig_ref[...] = result.astype(BF16)

        for copy in z_copies:
            copy.wait_send()

    for k in range(2):
        for peer in peers:

            @pl.when(needed(me, lax.rem(peer, Q)))
            def _(k=k, peer=peer):
                gather_copy(k, peer, me).wait_send()

            @pl.when(needed(peer, qb))
            def _(k=k, peer=peer):
                reduce_copy(k, peer, me).wait_send()


def scoped_kernel(sizes, *refs):
    L, H, Q, r, R, S, D, hd, G, chunks, kb, line, band = sizes
    n = L * Q
    sends = 2 * (D // H // 256) if line else H - 1
    dma = pltpu.SemaphoreType.DMA
    counts = [3 + 3 * chunks, 2 * n, 2 * n, 2 * n, 2 * n, sends, sends]
    counts += [3, 3, 2 + L, 2 + L, 2, 2, 2, 2]
    pl.run_scoped(lambda *sems: backward_kernel(sizes, *refs, *sems), *[dma((c,)) for c in counts])


def write_kernel(qg_in, ig_in, qg_out, ig_out, sems):
    copies = [
        pltpu.make_async_copy(qg_in, qg_out, sems.at[0]),
        pltpu.make_async_copy(ig_in, ig_out, sems.at[1]),
    ]
    for copy in copies:
        copy.start()
    for copy in copies:
        copy.wait()


def solution(mesh):
    L, H, Q = mesh.shape["layer"], mesh.shape["head"], mesh.shape["qblk"]
    n = L * Q

    def local(inputs, key_weight, value_weight, queries, output_cotangent, documents):
        r, D = inputs.shape
        hd = key_weight.shape[1]
        _, R, wide = queries.shape
        G = wide // hd
        S = documents.shape[0]
        chunks = D // 1024 if D % 1024 == 0 else 4
        kb = min(S, 384)
        line_mesh = L == 4 and H == 4 and Q == 2
        band = r if line_mesh and S == 2 * R and R % r == 0 and r % 16 == 0 else 0
        line = line_mesh and (D // H) % 256 == 0
        sizes = (L, H, Q, r, R, S, D, hd, G, chunks, kb, line, band)
        width = D // H
        streams = (2, width // 256, r, 256) if line else (H - 1, r, width)
        far_rows = width if line else 16
        cols = G * R
        tile = (R // band, S // 2 + band, G * band) if band else (S, cols)
        anywhere = pl.BlockSpec(memory_space=pl.ANY)
        vmem = pl.BlockSpec(memory_space=pltpu.VMEM)
        dma = pltpu.SemaphoreType.DMA
        query_grad, input_grad = pl.pallas_call(
            functools.partial(scoped_kernel, sizes),
            out_shape=(
                pltpu.VMEM(queries.shape, BF16),
                pltpu.VMEM((r, D // H), BF16),
            ),
            in_specs=[anywhere] * 6,
            out_specs=(vmem, vmem),
            scratch_shapes=[
                pltpu.VMEM((r, D), BF16),
                pltpu.VMEM((D, 2 * hd), BF16),
                pltpu.VMEM((cols, hd), BF16),
                pltpu.VMEM((cols, hd), BF16),
                pltpu.VMEM((2, n, r, hd), BF16),
                pltpu.VMEM((2, S, hd), BF16),
                pltpu.VMEM(tile, F32),
                pltpu.VMEM(tile if not band else (8, 128), F32),
                pltpu.VMEM(tile, BF16),
                pltpu.VMEM((2, S, hd) if band else (2, 8, hd), F32),
                pltpu.VMEM((2, n, r, hd), BF16),
                pltpu.VMEM((2, n, r, hd), BF16),
                pltpu.VMEM(streams, BF16),
                pltpu.VMEM(streams, BF16),
                pltpu.VMEM((2, far_rows, 2 * hd), BF16),
                pltpu.VMEM((2, r, 2 * hd), BF16),
                pltpu.VMEM((r, 2 * hd), BF16),
                pltpu.VMEM((r, width), F32),
                pltpu.VMEM((2, r, hd), BF16),
                pltpu.VMEM((S,), jnp.int32),
            ],
            compiler_params=pltpu.CompilerParams(
                collective_id=0, has_side_effects=True, vmem_limit_bytes=60 * 1024 * 1024
            ),
        )(
            inputs,
            key_weight,
            value_weight,
            queries,
            output_cotangent,
            documents,
        )
        return pl.pallas_call(
            write_kernel,
            out_shape=(
                jax.ShapeDtypeStruct(query_grad.shape, BF16),
                jax.ShapeDtypeStruct(input_grad.shape, BF16),
            ),
            in_specs=[vmem] * 2,
            out_specs=(anywhere, anywhere),
            scratch_shapes=[dma((2,))],
            compiler_params=pltpu.CompilerParams(vmem_limit_bytes=1024 * 1024),
        )(query_grad, input_grad)

    placed = (
        P(("layer", "qblk"), None),
        P(None, "head"),
        P(None, "head"),
        P("layer", "qblk", "head"),
        P("layer", "qblk", "head"),
        P(),
    )
    return jax.shard_map(
        local,
        mesh=mesh,
        in_specs=placed,
        out_specs=(P("layer", "qblk", "head"), P(("layer", "qblk"), "head")),
        check_vma=False,
    )
```

```python
import functools

import jax
import jax.numpy as jnp
from jax import lax
from jax.experimental import pallas as pl
from jax.experimental.pallas import tpu as pltpu
from jax.sharding import PartitionSpec as P

MESH = pl.DeviceIdType.MESH
NT = (((1,), (1,)), ((), ()))
TN = (((0,), (0,)), ((), ()))
F32 = jnp.float32
BF16 = jnp.bfloat16


def backward_kernel(
    sizes,
    x_hbm,
    wk_hbm,
    wv_hbm,
    q_hbm,
    g_hbm,
    docs_hbm,
    qg_ref,
    ig_ref,
    x_v,
    w_v,
    qf,
    gf,
    kv,
    kvf,
    st,
    dpt,
    ds16,
    acc_kv,
    sbuf,
    rbuf,
    zsend,
    zrecv,
    far_w,
    far_kv,
    own_kv,
    total,
    own_v,
    docs_ref,
    load_sem,
    ag_send,
    ag_recv,
    rs_send,
    rs_recv,
    z_send,
    z_recv,
    wz_send,
    wz_recv,
    wx_send,
    wx_recv,
    wt_send,
    wt_recv,
    kv_send,
    kv_recv,
):
    L, H, Q, r, R, S, D, hd, G, chunks, kb, line, band = sizes
    n = L * Q
    scaling = hd ** (-0.5)
    span = S // 2
    ly = lax.axis_index("layer")
    hh = lax.axis_index("head")
    qb = lax.axis_index("qblk")
    me = ly * Q + qb

    def needed(owner, block):
        above = owner * r < (block + 1) * R
        below = (owner + 1) * r - 1 >= block * R - span + 1
        return jnp.logical_and(above, below)

    def place(peer):
        return (peer // Q, hh, lax.rem(peer, Q))

    if L == 4 and Q == 2:
        row, col = ly // 2, lax.rem(ly, 2)
        far_layer = (1 - row) * 2 + 1 - col
        next_layers = [row * 2 + 1 - col, (1 - row) * 2 + col]
        peers = [far_layer * Q + qb, far_layer * Q + 1 - qb]
        peers += [layer * Q + qb for layer in next_layers]
        peers += [layer * Q + 1 - qb for layer in next_layers]
        peers += [ly * Q + 1 - qb]
    else:
        peers = [lax.rem(me + o, n) for o in range(1, n)]
    heads = [lax.rem(hh + o, H) for o in range(1, H)]

    barrier = pltpu.get_barrier_semaphore()
    for other in heads:
        pl.semaphore_signal(barrier, inc=1, device_id=(ly, other, qb), device_id_type=MESH)
    for peer in peers:
        pl.semaphore_signal(barrier, inc=1, device_id=place(peer), device_id_type=MESH)

    step = D // chunks
    loads = []
    for c in range(chunks):
        rows = pl.ds(c * step, step)
        loads.append(
            pltpu.make_async_copy(x_hbm.at[:, rows], x_v.at[:, rows], load_sem.at[3 * c])
        )
        loads.append(
            pltpu.make_async_copy(
                wk_hbm.at[rows, :], w_v.at[rows, pl.ds(0, hd)], load_sem.at[3 * c + 1]
            )
        )
        loads.append(
            pltpu.make_async_copy(
                wv_hbm.at[rows, :], w_v.at[rows, pl.ds(hd, hd)], load_sem.at[3 * c + 2]
            )
        )
    base = 3 * chunks
    docs_load = pltpu.make_async_copy(docs_hbm, docs_ref, load_sem.at[base + 2])
    docs_load.start()
    parts = R // band if band else 1
    tall = R // parts
    for i in range(parts):
        for g in range(G):
            cols = pl.ds(g * hd, hd)
            take = pl.ds(i * tall, tall)
            rows = pl.ds((i * G + g) * tall, tall)
            loads.append(
                pltpu.make_async_copy(q_hbm.at[0, take, cols], qf.at[rows, :], load_sem.at[base])
            )
            loads.append(
                pltpu.make_async_copy(
                    g_hbm.at[0, take, cols], gf.at[rows, :], load_sem.at[base + 1]
                )
            )
    for load in loads:
        load.start()

    acc = jnp.zeros((r, 2 * hd), F32)
    for c in range(chunks):
        for load in loads[3 * c : 3 * c + 3]:
            load.wait()
        acc = acc + jnp.dot(
            x_v[:, c * step : (c + 1) * step],
            w_v[c * step : (c + 1) * step, :],
            preferred_element_type=F32,
        )
    mine = acc.astype(BF16)
    for k in range(2):
        own_v[k] = mine[:, k * hd : (k + 1) * hd]
    pl.semaphore_wait(barrier, n - 1 + H - 1)

    def gather_copy(k, peer, slot):
        return pltpu.make_async_remote_copy(
            src_ref=own_v.at[k],
            dst_ref=kv.at[k, slot],
            send_sem=ag_send.at[k * n + peer],
            recv_sem=ag_recv.at[k * n + slot],
            device_id=place(peer),
            device_id_type=MESH,
        )

    for k in range(2):
        for peer in peers:

            @pl.when(needed(me, lax.rem(peer, Q)))
            def _(k=k, peer=peer):
                gather_copy(k, peer, me).start()

    width = D // H
    if line:
        half = width // Q
        piece = half // L
        wide = 256
        pieces = width // wide
        at_edge = jnp.logical_or(hh == 0, hh == 3)
        near = hh + 1 - 2 * lax.rem(hh, 2)
        second = lax.rem(hh + 2, 4)
        opposite = 3 - hh

        column = lax.rem(ly, 2)
        spots = [ly, column, 2 + ly // 2]
        beside = [ly + 1 - 2 * column, lax.rem(ly + 2, L)]

        def piece_rows(first, spot):
            return pl.ds(pl.multiple_of(first + qb * half + spot * piece, piece), piece)

        def prefetch(way, head):
            return pltpu.make_async_remote_copy(
                src_ref=w_v.at[piece_rows(head * width, spots[way]), :],
                dst_ref=far_w.at[min(way, 1), piece_rows(0, spots[way]), :],
                send_sem=wz_send.at[way],
                recv_sem=wz_recv.at[way],
                device_id=(ly, head, qb),
                device_id_type=MESH,
            )

        def share(layer, source):
            return pltpu.make_async_remote_copy(
                src_ref=far_w.at[0, piece_rows(0, source), :],
                dst_ref=far_w.at[0, piece_rows(0, source), :],
                send_sem=wx_send.at[layer],
                recv_sem=wx_recv.at[source],
                device_id=(layer, hh, qb),
                device_id_type=MESH,
            )

        def swap(way, spot):
            return pltpu.make_async_remote_copy(
                src_ref=far_w.at[1, piece_rows(0, spot), :],
                dst_ref=far_w.at[1, piece_rows(0, spot), :],
                send_sem=wx_send.at[L + way],
                recv_sem=wx_recv.at[L + way],
                device_id=(beside[way], hh, qb),
                device_id_type=MESH,
            )

        def twin(slot, spot, side):
            rows = pl.ds(pl.multiple_of(side * half + spot * piece, piece), piece)
            return pltpu.make_async_remote_copy(
                src_ref=far_w.at[slot, rows, :],
                dst_ref=far_w.at[slot, rows, :],
                send_sem=wt_send.at[slot * L + spot],
                recv_sem=wt_recv.at[slot * L + spot],
                device_id=(ly, hh, 1 - qb),
                device_id_type=MESH,
            )

        other_layers = [lax.rem(ly + o, L) for o in range(1, L)]

        prefetch(0, second).start()

    @pl.when(needed(me, qb))
    def _():
        for k in range(2):
            kv[k, me] = mine[:, k * hd : (k + 1) * hd]

    blank = jnp.zeros((r, hd), BF16)
    for d in range(n):

        @pl.when(jnp.logical_not(needed(d, qb)))
        def _(d=d):
            kv[0, d] = blank
            kv[1, d] = blank

        @pl.when(jnp.logical_not(needed(me, d % Q)))
        def _(d=d):
            rbuf[0, d] = blank
            rbuf[1, d] = blank

    docs_load.wait()
    docs = docs_ref[...].reshape(1, S)
    own_docs = docs[:, 0:R]
    for b in range(1, Q):
        own_docs = jnp.where(qb == b, docs[:, b * R : (b + 1) * R], own_docs)
    key_docs = jnp.transpose(jnp.broadcast_to(docs, (128, S)))[:, 0:1]
    first_key = jnp.sum((key_docs < own_docs).astype(F32), axis=0, keepdims=True).astype(jnp.int32)
    position = qb * R + lax.broadcasted_iota(jnp.int32, (1, R), 1)
    if band:
        first_keys = []
        positions = []
        for i in range(parts):
            take = slice(i * tall, (i + 1) * tall)
            first_keys.append(jnp.concatenate([first_key[:, take]] * G, axis=1))
            positions.append(jnp.concatenate([position[:, take]] * G, axis=1))
    else:
        first_key = jnp.concatenate([first_key] * G, axis=1)
        position = jnp.concatenate([position] * G, axis=1)

    pltpu.make_async_copy(qf, qf, load_sem.at[base]).wait()
    pltpu.make_async_copy(gf, gf, load_sem.at[base + 1]).wait()

    def gathered(k):
        for peer in peers:

            @pl.when(needed(peer, qb))
            def _(peer=peer):
                gather_copy(k, peer, peer).wait_recv()

        if r % 16 == 0:
            kvf[k] = kv[k].reshape(S, hd)
        else:
            for d in range(n):
                kvf[k, d * r : (d + 1) * r, :] = kv[k, d]

    gathered(0)
    if line:

        @pl.when(at_edge)
        def _():
            prefetch(1, opposite).start()
            prefetch(2, opposite).start()


    def reduce_copy(k, peer, slot):
        return pltpu.make_async_remote_copy(
            src_ref=sbuf.at[k, peer],
            dst_ref=rbuf.at[k, slot],
            send_sem=rs_send.at[k * n + peer],
            recv_sem=rs_recv.at[k * n + slot],
            device_id=place(peer),
            device_id_type=MESH,
        )

    def scatter(k):
        for peer in peers:

            @pl.when(needed(peer, qb))
            def _(peer=peer):
                reduce_copy(k, peer, me).start()

        @pl.when(needed(me, qb))
        def _():
            rbuf[k, me] = sbuf[k, me]

    if band:
        high = span + tall
        wide_cols = G * tall
        starts = [
            pl.multiple_of(jnp.maximum(qb * R + i * tall - span, 0), tall) for i in range(parts)
        ]
        windows = [pl.ds(start, high) for start in starts]
        takes = [slice(i * wide_cols, (i + 1) * wide_cols) for i in range(parts)]

        def hand_over(k, factor):
            for d in range(n):
                grad = acc_kv[k, d * r : (d + 1) * r, :]
                sbuf[k, d] = (grad * factor if factor else grad).astype(BF16)

        acc_kv[...] = jnp.zeros(acc_kv.shape, F32)
        tops = []
        for i in range(parts):
            key_pos = starts[i] + lax.broadcasted_iota(jnp.int32, (high, wide_cols), 0)
            visible = (key_pos >= first_keys[i]) & (key_pos <= positions[i])
            s = lax.dot_general(
                kvf[0, windows[i], :], qf[takes[i], :], NT, preferred_element_type=F32
            )
            s = jnp.where(visible, s * scaling, -1e30)
            st[i] = s
            tops.append(jnp.max(s, axis=0, keepdims=True))
        for i in range(parts):
            p = jnp.exp(st[i] - tops[i])
            p = p * (1.0 / jnp.sum(p, axis=0, keepdims=True))
            st[i] = p
            acc_kv[1, windows[i], :] += jnp.dot(
                p.astype(BF16), gf[takes[i], :], preferred_element_type=F32
            )
        hand_over(1, None)
        scatter(1)
        gathered(1)
        for i in range(parts):
            grad = lax.dot_general(
                kvf[1, windows[i], :], gf[takes[i], :], NT, preferred_element_type=F32
            )
            p = st[i]
            delta = jnp.sum(p * grad, axis=0, keepdims=True)
            ds = (p * (grad - delta)).astype(BF16)
            ds16[i] = ds
            acc_kv[0, windows[i], :] += jnp.dot(ds, qf[takes[i], :], preferred_element_type=F32)
        hand_over(0, scaling)
        scatter(0)
        for i in range(parts):
            dq = scaling * lax.dot_general(
                ds16[i], kvf[0, windows[i], :], TN, preferred_element_type=F32
            )
            for g in range(G):
                qg_ref[0, i * tall : (i + 1) * tall, g * hd : (g + 1) * hd] = dq[
                    g * tall : (g + 1) * tall
                ].astype(BF16)
    else:
        cols = G * R
        blocks = S // kb

        def run(body, carry):
            if blocks == 1:
                return body(0, carry)
            return lax.fori_loop(0, blocks, body, carry)

        def rows_of(j):
            return pl.ds(pl.multiple_of(j * kb, kb), kb) if blocks > 1 else pl.ds(0, kb)

        def scores(j, top):
            rows = rows_of(j)
            key_pos = j * kb + lax.broadcasted_iota(jnp.int32, (kb, cols), 0)
            visible = (key_pos >= first_key) & (key_pos <= position)
            s = lax.dot_general(kvf[0, rows, :], qf[...], NT, preferred_element_type=F32) * scaling
            s = jnp.where(visible, s, -1e30)
            st[rows, :] = s
            return jnp.maximum(top, jnp.max(s, axis=0, keepdims=True))

        top = run(scores, jnp.full((1, cols), -1e30, F32))

        def totals(j, total):
            rows = rows_of(j)
            p = jnp.exp(st[rows, :] - top)
            st[rows, :] = p
            return total + jnp.sum(p, axis=0, keepdims=True)

        zero_row = jnp.zeros((1, cols), F32)
        inverse = 1.0 / run(totals, zero_row)

        def keep(k, j, grad):
            grad = grad.astype(BF16)
            if blocks == 1:
                sbuf[k] = grad.reshape(n, r, hd)
            else:
                per = kb // r
                for i in range(per):
                    sbuf[k, j * per + i] = grad[i * r : (i + 1) * r]

        def value_grads(j, carry):
            rows = rows_of(j)
            p = st[rows, :] * inverse
            st[rows, :] = p
            keep(1, j, jnp.dot(p.astype(BF16), gf[...], preferred_element_type=F32))
            return carry

        run(value_grads, 0)
        scatter(1)
        gathered(1)

        def dots(j, dot):
            rows = rows_of(j)
            grad = lax.dot_general(kvf[1, rows, :], gf[...], NT, preferred_element_type=F32)
            dpt[rows, :] = grad
            return dot + jnp.sum(st[rows, :] * grad, axis=0, keepdims=True)

        delta = run(dots, zero_row)

        def key_grads(j, carry):
            rows = rows_of(j)
            ds = (st[rows, :] * (dpt[rows, :] - delta)).astype(BF16)
            ds16[rows, :] = ds
            keep(0, j, jnp.dot(ds, qf[...], preferred_element_type=F32) * scaling)
            return carry

        run(key_grads, 0)
        scatter(0)

        def query_grads(j, carry):
            rows = rows_of(j)
            return carry + lax.dot_general(
                ds16[rows, :], kvf[0, rows, :], TN, preferred_element_type=F32
            )

        dq = run(query_grads, jnp.zeros((cols, hd), F32)) * scaling
        for g in range(G):
            qg_ref[0, :, g * hd : (g + 1) * hd] = dq[g * R : (g + 1) * R].astype(BF16)

    if line:

        def start_sharing():
            prefetch(0, second).wait_recv()
            for layer in other_layers:
                share(layer, ly).start()
            twin(0, ly, qb).start()

        pl.when(at_edge)(start_sharing)

    for k in (1, 0):
        for peer in peers:

            @pl.when(needed(me, lax.rem(peer, Q)))
            def _(k=k, peer=peer):
                reduce_copy(k, peer, peer).wait_recv()

    halves = []
    for k in range(2):
        owned = rbuf[k, 0].astype(F32)
        for d in range(1, n):
            owned = owned + rbuf[k, d].astype(F32)
        halves.append(owned.astype(BF16))
    owned = jnp.concatenate(halves, axis=1)

    def part_of(head):
        rows = pl.ds(pl.multiple_of(head * width, width), width)
        return lax.dot_general(owned, w_v[rows, :], NT, preferred_element_type=F32)

    if line:
        own_kv[...] = owned

        def chunk_of(head, c):
            rows = pl.ds(pl.multiple_of(head * width + c * wide, wide), wide)
            return lax.dot_general(owned, w_v[rows, :], NT, preferred_element_type=F32)

        def far_chunk(slot, c):
            return lax.dot_general(
                far_kv[slot],
                far_w[slot, c * wide : (c + 1) * wide, :],
                NT,
                preferred_element_type=F32,
            )

        def factor(slot, head):
            return pltpu.make_async_remote_copy(
                src_ref=own_kv,
                dst_ref=far_kv.at[slot],
                send_sem=kv_send.at[slot],
                recv_sem=kv_recv.at[slot],
                device_id=(ly, head, qb),
                device_id_type=MESH,
            )

        def stream(k, c, head):
            return pltpu.make_async_remote_copy(
                src_ref=zsend.at[k, c],
                dst_ref=zrecv.at[k, c],
                send_sem=z_send.at[k * pieces + c],
                recv_sem=z_recv.at[k * pieces + c],
                device_id=(ly, head, qb),
                device_id_type=MESH,
            )

        @pl.when(at_edge)
        def _():
            factor(1, opposite).start()

        factor(0, second).start()

        @pl.when(jnp.logical_not(at_edge))
        def _():
            start_sharing()
            for c in range(pieces):
                zsend[1, c] = chunk_of(opposite, c).astype(BF16)
                stream(1, c, opposite).start()

        for c in range(pieces):
            zsend[0, c] = chunk_of(near, c).astype(BF16)
            stream(0, c, near).start()

        for c in range(pieces):
            total[:, c * wide : (c + 1) * wide] = chunk_of(hh, c)

        @pl.when(at_edge)
        def _():
            for way in (1, 2):
                prefetch(way, opposite).wait_recv()
                swap(way - 1, spots[way]).start()
                twin(1, spots[way], qb).start()

        for layer in other_layers:
            share(layer, layer).wait_recv()
            twin(0, layer, qb).start()

        factor(0, second).wait_recv()
        for spot in range(L):
            twin(0, spot, 1 - qb).wait_recv()
        for c in range(pieces):
            total[:, c * wide : (c + 1) * wide] += far_chunk(0, c)

        @pl.when(at_edge)
        def _():
            for way, spot in enumerate((1 - column, 3 - ly // 2)):
                swap(way, spot).wait_recv()
                twin(1, spot, qb).start()

        @pl.when(at_edge)
        def _():
            factor(1, opposite).wait_recv()
            for spot in range(L):
                twin(1, spot, 1 - qb).wait_recv()
            for c in range(pieces):
                total[:, c * wide : (c + 1) * wide] += far_chunk(1, c)

        @pl.when(jnp.logical_not(at_edge))
        def _():
            for c in range(pieces):
                stream(1, c, opposite).wait_recv()
                total[:, c * wide : (c + 1) * wide] += zrecv[1, c].astype(F32)

        for c in range(pieces):
            stream(0, c, near).wait_recv()
            cols_c = slice(c * wide, (c + 1) * wide)
            ig_ref[:, cols_c] = (total[:, cols_c] + zrecv[0, c].astype(F32)).astype(BF16)

        @pl.when(at_edge)
        def _():
            for way in (1, 2):
                prefetch(way, opposite).wait_send()
                swap(way - 1, spots[way]).wait_send()
            for spot in range(L):
                twin(1, spot, qb).wait_send()
            factor(1, opposite).wait_send()

        @pl.when(jnp.logical_not(at_edge))
        def _():
            for c in range(pieces):
                stream(1, c, opposite).wait_send()

        prefetch(0, second).wait_send()
        for layer in other_layers:
            share(layer, ly).wait_send()
        for spot in range(L):
            twin(0, spot, qb).wait_send()
        factor(0, second).wait_send()
        for c in range(pieces):
            stream(0, c, near).wait_send()
    else:
        z_copies = []
        for o in range(1, H):
            other = heads[o - 1]
            zsend[o - 1] = part_of(other).astype(BF16)
            copy = pltpu.make_async_remote_copy(
                src_ref=zsend.at[o - 1],
                dst_ref=zrecv.at[o - 1],
                send_sem=z_send.at[o - 1],
                recv_sem=z_recv.at[o - 1],
                device_id=(ly, other, qb),
                device_id_type=MESH,
            )
            copy.start()
            z_copies.append(copy)
        result = part_of(hh)
        for o, copy in enumerate(z_copies):
            copy.wait_recv()
            result = result + zrecv[o].astype(F32)
        ig_ref[...] = result.astype(BF16)

        for copy in z_copies:
            copy.wait_send()

    for k in range(2):
        for peer in peers:

            @pl.when(needed(me, lax.rem(peer, Q)))
            def _(k=k, peer=peer):
                gather_copy(k, peer, me).wait_send()

            @pl.when(needed(peer, qb))
            def _(k=k, peer=peer):
                reduce_copy(k, peer, me).wait_send()


def scoped_kernel(sizes, *refs):
    L, H, Q, r, R, S, D, hd, G, chunks, kb, line, band = sizes
    n = L * Q
    sends = 2 * (D // H // 256) if line else H - 1
    dma = pltpu.SemaphoreType.DMA
    counts = [3 + 3 * chunks, 2 * n, 2 * n, 2 * n, 2 * n, sends, sends]
    counts += [3, 3, 2 + L, 2 + L, 2 * L, 2 * L, 2, 2]
    pl.run_scoped(lambda *sems: backward_kernel(sizes, *refs, *sems), *[dma((c,)) for c in counts])


def write_kernel(qg_in, ig_in, qg_out, ig_out, sems):
    copies = [
        pltpu.make_async_copy(qg_in, qg_out, sems.at[0]),
        pltpu.make_async_copy(ig_in, ig_out, sems.at[1]),
    ]
    for copy in copies:
        copy.start()
    for copy in copies:
        copy.wait()


def solution(mesh):
    L, H, Q = mesh.shape["layer"], mesh.shape["head"], mesh.shape["qblk"]
    n = L * Q

    def local(inputs, key_weight, value_weight, queries, output_cotangent, documents):
        r, D = inputs.shape
        hd = key_weight.shape[1]
        _, R, wide = queries.shape
        G = wide // hd
        S = documents.shape[0]
        chunks = D // 1024 if D % 1024 == 0 else 4
        kb = min(S, 384)
        line_mesh = L == 4 and H == 4 and Q == 2
        band = r if line_mesh and S == 2 * R and R % r == 0 and r % 16 == 0 else 0
        line = line_mesh and (D // H) % 256 == 0
        sizes = (L, H, Q, r, R, S, D, hd, G, chunks, kb, line, band)
        width = D // H
        streams = (2, width // 256, r, 256) if line else (H - 1, r, width)
        far_rows = width if line else 16
        cols = G * R
        tile = (R // band, S // 2 + band, G * band) if band else (S, cols)
        anywhere = pl.BlockSpec(memory_space=pl.ANY)
        vmem = pl.BlockSpec(memory_space=pltpu.VMEM)
        dma = pltpu.SemaphoreType.DMA
        query_grad, input_grad = pl.pallas_call(
            functools.partial(scoped_kernel, sizes),
            out_shape=(
                pltpu.VMEM(queries.shape, BF16),
                pltpu.VMEM((r, D // H), BF16),
            ),
            in_specs=[anywhere] * 6,
            out_specs=(vmem, vmem),
            scratch_shapes=[
                pltpu.VMEM((r, D), BF16),
                pltpu.VMEM((D, 2 * hd), BF16),
                pltpu.VMEM((cols, hd), BF16),
                pltpu.VMEM((cols, hd), BF16),
                pltpu.VMEM((2, n, r, hd), BF16),
                pltpu.VMEM((2, S, hd), BF16),
                pltpu.VMEM(tile, F32),
                pltpu.VMEM(tile if not band else (8, 128), F32),
                pltpu.VMEM(tile, BF16),
                pltpu.VMEM((2, S, hd) if band else (2, 8, hd), F32),
                pltpu.VMEM((2, n, r, hd), BF16),
                pltpu.VMEM((2, n, r, hd), BF16),
                pltpu.VMEM(streams, BF16),
                pltpu.VMEM(streams, BF16),
                pltpu.VMEM((2, far_rows, 2 * hd), BF16),
                pltpu.VMEM((2, r, 2 * hd), BF16),
                pltpu.VMEM((r, 2 * hd), BF16),
                pltpu.VMEM((r, width), F32),
                pltpu.VMEM((2, r, hd), BF16),
                pltpu.VMEM((S,), jnp.int32),
            ],
            compiler_params=pltpu.CompilerParams(
                collective_id=0, has_side_effects=True, vmem_limit_bytes=60 * 1024 * 1024
            ),
        )(
            inputs,
            key_weight,
            value_weight,
            queries,
            output_cotangent,
            documents,
        )
        return pl.pallas_call(
            write_kernel,
            out_shape=(
                jax.ShapeDtypeStruct(query_grad.shape, BF16),
                jax.ShapeDtypeStruct(input_grad.shape, BF16),
            ),
            in_specs=[vmem] * 2,
            out_specs=(anywhere, anywhere),
            scratch_shapes=[dma((2,))],
            compiler_params=pltpu.CompilerParams(vmem_limit_bytes=1024 * 1024),
        )(query_grad, input_grad)

    placed = (
        P(("layer", "qblk"), None),
        P(None, "head"),
        P(None, "head"),
        P("layer", "qblk", "head"),
        P("layer", "qblk", "head"),
        P(),
    )
    return jax.shard_map(
        local,
        mesh=mesh,
        in_specs=placed,
        out_specs=(P("layer", "qblk", "head"), P(("layer", "qblk"), "head")),
        check_vma=False,
    )
```

```python
import functools

import jax
import jax.numpy as jnp
from jax import lax
from jax.experimental import pallas as pl
from jax.experimental.pallas import tpu as pltpu
from jax.sharding import PartitionSpec as P

MESH = pl.DeviceIdType.MESH
NT = (((1,), (1,)), ((), ()))
TN = (((0,), (0,)), ((), ()))
F32 = jnp.float32
BF16 = jnp.bfloat16


def backward_kernel(
    sizes,
    x_hbm,
    wk_hbm,
    wv_hbm,
    q_hbm,
    g_hbm,
    docs_hbm,
    qg_ref,
    ig_ref,
    x_v,
    w_v,
    qf,
    gf,
    kv,
    kvf,
    st,
    dpt,
    ds16,
    acc_kv,
    sbuf,
    rbuf,
    zsend,
    zrecv,
    far_w,
    far_kv,
    own_kv,
    total,
    own_v,
    docs_ref,
    load_sem,
    ag_send,
    ag_recv,
    rs_send,
    rs_recv,
    z_send,
    z_recv,
    wz_send,
    wz_recv,
    wx_send,
    wx_recv,
    wt_send,
    wt_recv,
    kv_send,
    kv_recv,
):
    L, H, Q, r, R, S, D, hd, G, chunks, kb, line, band = sizes
    n = L * Q
    scaling = hd ** (-0.5)
    span = S // 2
    ly = lax.axis_index("layer")
    hh = lax.axis_index("head")
    qb = lax.axis_index("qblk")
    me = ly * Q + qb

    def needed(owner, block):
        above = owner * r < (block + 1) * R
        below = (owner + 1) * r - 1 >= block * R - span + 1
        return jnp.logical_and(above, below)

    def place(peer):
        return (peer // Q, hh, lax.rem(peer, Q))

    if L == 4 and Q == 2:
        row, col = ly // 2, lax.rem(ly, 2)
        far_layer = (1 - row) * 2 + 1 - col
        next_layers = [row * 2 + 1 - col, (1 - row) * 2 + col]
        peers = [far_layer * Q + qb, far_layer * Q + 1 - qb]
        peers += [layer * Q + qb for layer in next_layers]
        peers += [layer * Q + 1 - qb for layer in next_layers]
        peers += [ly * Q + 1 - qb]
    else:
        peers = [lax.rem(me + o, n) for o in range(1, n)]
    heads = [lax.rem(hh + o, H) for o in range(1, H)]

    barrier = pltpu.get_barrier_semaphore()
    for other in heads:
        pl.semaphore_signal(barrier, inc=1, device_id=(ly, other, qb), device_id_type=MESH)
    for peer in peers:
        pl.semaphore_signal(barrier, inc=1, device_id=place(peer), device_id_type=MESH)

    step = D // chunks
    loads = []
    for c in range(chunks):
        rows = pl.ds(c * step, step)
        loads.append(
            pltpu.make_async_copy(x_hbm.at[:, rows], x_v.at[:, rows], load_sem.at[3 * c])
        )
        loads.append(
            pltpu.make_async_copy(
                wk_hbm.at[rows, :], w_v.at[rows, pl.ds(0, hd)], load_sem.at[3 * c + 1]
            )
        )
        loads.append(
            pltpu.make_async_copy(
                wv_hbm.at[rows, :], w_v.at[rows, pl.ds(hd, hd)], load_sem.at[3 * c + 2]
            )
        )
    base = 3 * chunks
    docs_load = pltpu.make_async_copy(docs_hbm, docs_ref, load_sem.at[base + 2])
    docs_load.start()
    parts = R // band if band else 1
    tall = R // parts
    for i in range(parts):
        for g in range(G):
            cols = pl.ds(g * hd, hd)
            take = pl.ds(i * tall, tall)
            rows = pl.ds((i * G + g) * tall, tall)
            loads.append(
                pltpu.make_async_copy(q_hbm.at[0, take, cols], qf.at[rows, :], load_sem.at[base])
            )
            loads.append(
                pltpu.make_async_copy(
                    g_hbm.at[0, take, cols], gf.at[rows, :], load_sem.at[base + 1]
                )
            )
    for load in loads:
        load.start()

    acc = jnp.zeros((r, 2 * hd), F32)
    for c in range(chunks):
        for load in loads[3 * c : 3 * c + 3]:
            load.wait()
        acc = acc + jnp.dot(
            x_v[:, c * step : (c + 1) * step],
            w_v[c * step : (c + 1) * step, :],
            preferred_element_type=F32,
        )
    mine = acc.astype(BF16)
    for k in range(2):
        own_v[k] = mine[:, k * hd : (k + 1) * hd]
    pl.semaphore_wait(barrier, n - 1 + H - 1)

    def gather_copy(k, peer, slot):
        return pltpu.make_async_remote_copy(
            src_ref=own_v.at[k],
            dst_ref=kv.at[k, slot],
            send_sem=ag_send.at[k * n + peer],
            recv_sem=ag_recv.at[k * n + slot],
            device_id=place(peer),
            device_id_type=MESH,
        )

    for k in range(2):
        for peer in peers:

            @pl.when(needed(me, lax.rem(peer, Q)))
            def _(k=k, peer=peer):
                gather_copy(k, peer, me).start()

    width = D // H
    if line:
        half = width // Q
        piece = half // L
        wide = 256
        pieces = width // wide
        at_edge = jnp.logical_or(hh == 0, hh == 3)
        near = hh + 1 - 2 * lax.rem(hh, 2)
        second = lax.rem(hh + 2, 4)
        opposite = 3 - hh

        column = lax.rem(ly, 2)
        spots = [ly, column, 2 + ly // 2]
        beside = [ly + 1 - 2 * column, lax.rem(ly + 2, L)]

        def piece_rows(first, spot):
            return pl.ds(pl.multiple_of(first + qb * half + spot * piece, piece), piece)

        def prefetch(way, head):
            return pltpu.make_async_remote_copy(
                src_ref=w_v.at[piece_rows(head * width, spots[way]), :],
                dst_ref=far_w.at[min(way, 1), piece_rows(0, spots[way]), :],
                send_sem=wz_send.at[way],
                recv_sem=wz_recv.at[way],
                device_id=(ly, head, qb),
                device_id_type=MESH,
            )

        def share(layer, source):
            return pltpu.make_async_remote_copy(
                src_ref=far_w.at[0, piece_rows(0, source), :],
                dst_ref=far_w.at[0, piece_rows(0, source), :],
                send_sem=wx_send.at[layer],
                recv_sem=wx_recv.at[source],
                device_id=(layer, hh, qb),
                device_id_type=MESH,
            )

        def swap(way, spot):
            return pltpu.make_async_remote_copy(
                src_ref=far_w.at[1, piece_rows(0, spot), :],
                dst_ref=far_w.at[1, piece_rows(0, spot), :],
                send_sem=wx_send.at[L + way],
                recv_sem=wx_recv.at[L + way],
                device_id=(beside[way], hh, qb),
                device_id_type=MESH,
            )

        def twin(slot, spot, side):
            rows = pl.ds(pl.multiple_of(side * half + spot * piece, piece), piece)
            return pltpu.make_async_remote_copy(
                src_ref=far_w.at[slot, rows, :],
                dst_ref=far_w.at[slot, rows, :],
                send_sem=wt_send.at[slot * L + spot],
                recv_sem=wt_recv.at[slot * L + spot],
                device_id=(ly, hh, 1 - qb),
                device_id_type=MESH,
            )

        other_layers = [*beside, L - 1 - ly]

        prefetch(0, second).start()

    @pl.when(needed(me, qb))
    def _():
        for k in range(2):
            kv[k, me] = mine[:, k * hd : (k + 1) * hd]

    blank = jnp.zeros((r, hd), BF16)
    for d in range(n):

        @pl.when(jnp.logical_not(needed(d, qb)))
        def _(d=d):
            kv[0, d] = blank
            kv[1, d] = blank

        @pl.when(jnp.logical_not(needed(me, d % Q)))
        def _(d=d):
            rbuf[0, d] = blank
            rbuf[1, d] = blank

    docs_load.wait()
    docs = docs_ref[...].reshape(1, S)
    own_docs = docs[:, 0:R]
    for b in range(1, Q):
        own_docs = jnp.where(qb == b, docs[:, b * R : (b + 1) * R], own_docs)
    key_docs = jnp.transpose(jnp.broadcast_to(docs, (128, S)))[:, 0:1]
    first_key = jnp.sum((key_docs < own_docs).astype(F32), axis=0, keepdims=True).astype(jnp.int32)
    position = qb * R + lax.broadcasted_iota(jnp.int32, (1, R), 1)
    if band:
        first_keys = []
        positions = []
        for i in range(parts):
            take = slice(i * tall, (i + 1) * tall)
            first_keys.append(jnp.concatenate([first_key[:, take]] * G, axis=1))
            positions.append(jnp.concatenate([position[:, take]] * G, axis=1))
    else:
        first_key = jnp.concatenate([first_key] * G, axis=1)
        position = jnp.concatenate([position] * G, axis=1)

    pltpu.make_async_copy(qf, qf, load_sem.at[base]).wait()
    pltpu.make_async_copy(gf, gf, load_sem.at[base + 1]).wait()

    def gathered(k):
        for peer in peers:

            @pl.when(needed(peer, qb))
            def _(peer=peer):
                gather_copy(k, peer, peer).wait_recv()

        if r % 16 == 0:
            kvf[k] = kv[k].reshape(S, hd)
        else:
            for d in range(n):
                kvf[k, d * r : (d + 1) * r, :] = kv[k, d]

    gathered(0)
    if line:

        @pl.when(at_edge)
        def _():
            prefetch(1, opposite).start()
            prefetch(2, opposite).start()


    def reduce_copy(k, peer, slot):
        return pltpu.make_async_remote_copy(
            src_ref=sbuf.at[k, peer],
            dst_ref=rbuf.at[k, slot],
            send_sem=rs_send.at[k * n + peer],
            recv_sem=rs_recv.at[k * n + slot],
            device_id=place(peer),
            device_id_type=MESH,
        )

    def scatter(k):
        for peer in peers:

            @pl.when(needed(peer, qb))
            def _(peer=peer):
                reduce_copy(k, peer, me).start()

        @pl.when(needed(me, qb))
        def _():
            rbuf[k, me] = sbuf[k, me]

    if band:
        high = span + tall
        wide_cols = G * tall
        starts = [
            pl.multiple_of(jnp.maximum(qb * R + i * tall - span, 0), tall) for i in range(parts)
        ]
        windows = [pl.ds(start, high) for start in starts]
        takes = [slice(i * wide_cols, (i + 1) * wide_cols) for i in range(parts)]

        def hand_over(k, factor):
            for d in range(n):
                grad = acc_kv[k, d * r : (d + 1) * r, :]
                sbuf[k, d] = (grad * factor if factor else grad).astype(BF16)

        acc_kv[...] = jnp.zeros(acc_kv.shape, F32)
        tops = []
        for i in range(parts):
            key_pos = starts[i] + lax.broadcasted_iota(jnp.int32, (high, wide_cols), 0)
            visible = (key_pos >= first_keys[i]) & (key_pos <= positions[i])
            s = lax.dot_general(
                kvf[0, windows[i], :], qf[takes[i], :], NT, preferred_element_type=F32
            )
            s = jnp.where(visible, s * scaling, -1e30)
            st[i] = s
            tops.append(jnp.max(s, axis=0, keepdims=True))
        for i in range(parts):
            p = jnp.exp(st[i] - tops[i])
            p = p * (1.0 / jnp.sum(p, axis=0, keepdims=True))
            st[i] = p
            acc_kv[1, windows[i], :] += jnp.dot(
                p.astype(BF16), gf[takes[i], :], preferred_element_type=F32
            )
        hand_over(1, None)
        scatter(1)
        gathered(1)
        for i in range(parts):
            grad = lax.dot_general(
                kvf[1, windows[i], :], gf[takes[i], :], NT, preferred_element_type=F32
            )
            p = st[i]
            delta = jnp.sum(p * grad, axis=0, keepdims=True)
            ds = (p * (grad - delta)).astype(BF16)
            ds16[i] = ds
            acc_kv[0, windows[i], :] += jnp.dot(ds, qf[takes[i], :], preferred_element_type=F32)
        hand_over(0, scaling)
        scatter(0)
        for i in range(parts):
            dq = scaling * lax.dot_general(
                ds16[i], kvf[0, windows[i], :], TN, preferred_element_type=F32
            )
            for g in range(G):
                qg_ref[0, i * tall : (i + 1) * tall, g * hd : (g + 1) * hd] = dq[
                    g * tall : (g + 1) * tall
                ].astype(BF16)
    else:
        cols = G * R
        blocks = S // kb

        def run(body, carry):
            if blocks == 1:
                return body(0, carry)
            return lax.fori_loop(0, blocks, body, carry)

        def rows_of(j):
            return pl.ds(pl.multiple_of(j * kb, kb), kb) if blocks > 1 else pl.ds(0, kb)

        def scores(j, top):
            rows = rows_of(j)
            key_pos = j * kb + lax.broadcasted_iota(jnp.int32, (kb, cols), 0)
            visible = (key_pos >= first_key) & (key_pos <= position)
            s = lax.dot_general(kvf[0, rows, :], qf[...], NT, preferred_element_type=F32) * scaling
            s = jnp.where(visible, s, -1e30)
            st[rows, :] = s
            return jnp.maximum(top, jnp.max(s, axis=0, keepdims=True))

        top = run(scores, jnp.full((1, cols), -1e30, F32))

        def totals(j, total):
            rows = rows_of(j)
            p = jnp.exp(st[rows, :] - top)
            st[rows, :] = p
            return total + jnp.sum(p, axis=0, keepdims=True)

        zero_row = jnp.zeros((1, cols), F32)
        inverse = 1.0 / run(totals, zero_row)

        def keep(k, j, grad):
            grad = grad.astype(BF16)
            if blocks == 1:
                sbuf[k] = grad.reshape(n, r, hd)
            else:
                per = kb // r
                for i in range(per):
                    sbuf[k, j * per + i] = grad[i * r : (i + 1) * r]

        def value_grads(j, carry):
            rows = rows_of(j)
            p = st[rows, :] * inverse
            st[rows, :] = p
            keep(1, j, jnp.dot(p.astype(BF16), gf[...], preferred_element_type=F32))
            return carry

        run(value_grads, 0)
        scatter(1)
        gathered(1)

        def dots(j, dot):
            rows = rows_of(j)
            grad = lax.dot_general(kvf[1, rows, :], gf[...], NT, preferred_element_type=F32)
            dpt[rows, :] = grad
            return dot + jnp.sum(st[rows, :] * grad, axis=0, keepdims=True)

        delta = run(dots, zero_row)

        def key_grads(j, carry):
            rows = rows_of(j)
            ds = (st[rows, :] * (dpt[rows, :] - delta)).astype(BF16)
            ds16[rows, :] = ds
            keep(0, j, jnp.dot(ds, qf[...], preferred_element_type=F32) * scaling)
            return carry

        run(key_grads, 0)
        scatter(0)

        def query_grads(j, carry):
            rows = rows_of(j)
            return carry + lax.dot_general(
                ds16[rows, :], kvf[0, rows, :], TN, preferred_element_type=F32
            )

        dq = run(query_grads, jnp.zeros((cols, hd), F32)) * scaling
        for g in range(G):
            qg_ref[0, :, g * hd : (g + 1) * hd] = dq[g * R : (g + 1) * R].astype(BF16)

    if line:

        def start_sharing():
            prefetch(0, second).wait_recv()
            for layer in other_layers:
                share(layer, ly).start()
            twin(0, ly, qb).start()

        pl.when(at_edge)(start_sharing)

    for k in (1, 0):
        for peer in peers:

            @pl.when(needed(me, lax.rem(peer, Q)))
            def _(k=k, peer=peer):
                reduce_copy(k, peer, peer).wait_recv()

    halves = []
    for k in range(2):
        owned = rbuf[k, 0].astype(F32)
        for d in range(1, n):
            owned = owned + rbuf[k, d].astype(F32)
        halves.append(owned.astype(BF16))
    owned = jnp.concatenate(halves, axis=1)

    def part_of(head):
        rows = pl.ds(pl.multiple_of(head * width, width), width)
        return lax.dot_general(owned, w_v[rows, :], NT, preferred_element_type=F32)

    if line:
        own_kv[...] = owned

        def chunk_of(head, c):
            rows = pl.ds(pl.multiple_of(head * width + c * wide, wide), wide)
            return lax.dot_general(owned, w_v[rows, :], NT, preferred_element_type=F32)

        def far_chunk(slot, c):
            return lax.dot_general(
                far_kv[slot],
                far_w[slot, c * wide : (c + 1) * wide, :],
                NT,
                preferred_element_type=F32,
            )

        def factor(slot, head):
            return pltpu.make_async_remote_copy(
                src_ref=own_kv,
                dst_ref=far_kv.at[slot],
                send_sem=kv_send.at[slot],
                recv_sem=kv_recv.at[slot],
                device_id=(ly, head, qb),
                device_id_type=MESH,
            )

        def stream(k, c, head):
            return pltpu.make_async_remote_copy(
                src_ref=zsend.at[k, c],
                dst_ref=zrecv.at[k, c],
                send_sem=z_send.at[k * pieces + c],
                recv_sem=z_recv.at[k * pieces + c],
                device_id=(ly, head, qb),
                device_id_type=MESH,
            )

        @pl.when(at_edge)
        def _():
            factor(1, opposite).start()

        factor(0, second).start()

        @pl.when(jnp.logical_not(at_edge))
        def _():
            start_sharing()
            for c in range(pieces):
                zsend[1, c] = chunk_of(opposite, c).astype(BF16)
                stream(1, c, opposite).start()

        for c in range(pieces):
            zsend[0, c] = chunk_of(near, c).astype(BF16)
            stream(0, c, near).start()

        @pl.when(at_edge)
        def _():
            for way in (1, 2):
                prefetch(way, opposite).wait_recv()
                swap(way - 1, spots[way]).start()
                twin(1, spots[way], qb).start()

        for c in range(pieces):
            total[:, c * wide : (c + 1) * wide] = chunk_of(hh, c)

        for layer in other_layers:
            share(layer, layer).wait_recv()
            twin(0, layer, qb).start()

        factor(0, second).wait_recv()
        for spot in range(L):
            twin(0, spot, 1 - qb).wait_recv()
        for c in range(pieces):
            total[:, c * wide : (c + 1) * wide] += far_chunk(0, c)

        @pl.when(at_edge)
        def _():
            for way, spot in enumerate((1 - column, 3 - ly // 2)):
                swap(way, spot).wait_recv()
                twin(1, spot, qb).start()

        @pl.when(at_edge)
        def _():
            factor(1, opposite).wait_recv()
            for spot in range(L):
                twin(1, spot, 1 - qb).wait_recv()
            for c in range(pieces):
                total[:, c * wide : (c + 1) * wide] += far_chunk(1, c)

        @pl.when(jnp.logical_not(at_edge))
        def _():
            for c in range(pieces):
                stream(1, c, opposite).wait_recv()
                total[:, c * wide : (c + 1) * wide] += zrecv[1, c].astype(F32)

        for c in range(pieces):
            stream(0, c, near).wait_recv()
            cols_c = slice(c * wide, (c + 1) * wide)
            ig_ref[:, cols_c] = (total[:, cols_c] + zrecv[0, c].astype(F32)).astype(BF16)

        @pl.when(at_edge)
        def _():
            for way in (1, 2):
                prefetch(way, opposite).wait_send()
                swap(way - 1, spots[way]).wait_send()
            for spot in range(L):
                twin(1, spot, qb).wait_send()
            factor(1, opposite).wait_send()

        @pl.when(jnp.logical_not(at_edge))
        def _():
            for c in range(pieces):
                stream(1, c, opposite).wait_send()

        prefetch(0, second).wait_send()
        for layer in other_layers:
            share(layer, ly).wait_send()
        for spot in range(L):
            twin(0, spot, qb).wait_send()
        factor(0, second).wait_send()
        for c in range(pieces):
            stream(0, c, near).wait_send()
    else:
        z_copies = []
        for o in range(1, H):
            other = heads[o - 1]
            zsend[o - 1] = part_of(other).astype(BF16)
            copy = pltpu.make_async_remote_copy(
                src_ref=zsend.at[o - 1],
                dst_ref=zrecv.at[o - 1],
                send_sem=z_send.at[o - 1],
                recv_sem=z_recv.at[o - 1],
                device_id=(ly, other, qb),
                device_id_type=MESH,
            )
            copy.start()
            z_copies.append(copy)
        result = part_of(hh)
        for o, copy in enumerate(z_copies):
            copy.wait_recv()
            result = result + zrecv[o].astype(F32)
        ig_ref[...] = result.astype(BF16)

        for copy in z_copies:
            copy.wait_send()

    for k in range(2):
        for peer in peers:

            @pl.when(needed(me, lax.rem(peer, Q)))
            def _(k=k, peer=peer):
                gather_copy(k, peer, me).wait_send()

            @pl.when(needed(peer, qb))
            def _(k=k, peer=peer):
                reduce_copy(k, peer, me).wait_send()


def scoped_kernel(sizes, *refs):
    L, H, Q, r, R, S, D, hd, G, chunks, kb, line, band = sizes
    n = L * Q
    sends = 2 * (D // H // 256) if line else H - 1
    dma = pltpu.SemaphoreType.DMA
    counts = [3 + 3 * chunks, 2 * n, 2 * n, 2 * n, 2 * n, sends, sends]
    counts += [3, 3, 2 + L, 2 + L, 2 * L, 2 * L, 2, 2]
    pl.run_scoped(lambda *sems: backward_kernel(sizes, *refs, *sems), *[dma((c,)) for c in counts])


def write_kernel(qg_in, ig_in, qg_out, ig_out, sems):
    copies = [
        pltpu.make_async_copy(qg_in, qg_out, sems.at[0]),
        pltpu.make_async_copy(ig_in, ig_out, sems.at[1]),
    ]
    for copy in copies:
        copy.start()
    for copy in copies:
        copy.wait()


def solution(mesh):
    L, H, Q = mesh.shape["layer"], mesh.shape["head"], mesh.shape["qblk"]
    n = L * Q

    def local(inputs, key_weight, value_weight, queries, output_cotangent, documents):
        r, D = inputs.shape
        hd = key_weight.shape[1]
        _, R, wide = queries.shape
        G = wide // hd
        S = documents.shape[0]
        chunks = D // 1024 if D % 1024 == 0 else 4
        kb = min(S, 384)
        line_mesh = L == 4 and H == 4 and Q == 2
        band = r if line_mesh and S == 2 * R and R % r == 0 and r % 16 == 0 else 0
        line = line_mesh and (D // H) % 256 == 0
        sizes = (L, H, Q, r, R, S, D, hd, G, chunks, kb, line, band)
        width = D // H
        streams = (2, width // 256, r, 256) if line else (H - 1, r, width)
        far_rows = width if line else 16
        cols = G * R
        tile = (R // band, S // 2 + band, G * band) if band else (S, cols)
        anywhere = pl.BlockSpec(memory_space=pl.ANY)
        vmem = pl.BlockSpec(memory_space=pltpu.VMEM)
        dma = pltpu.SemaphoreType.DMA
        query_grad, input_grad = pl.pallas_call(
            functools.partial(scoped_kernel, sizes),
            out_shape=(
                pltpu.VMEM(queries.shape, BF16),
                pltpu.VMEM((r, D // H), BF16),
            ),
            in_specs=[anywhere] * 6,
            out_specs=(vmem, vmem),
            scratch_shapes=[
                pltpu.VMEM((r, D), BF16),
                pltpu.VMEM((D, 2 * hd), BF16),
                pltpu.VMEM((cols, hd), BF16),
                pltpu.VMEM((cols, hd), BF16),
                pltpu.VMEM((2, n, r, hd), BF16),
                pltpu.VMEM((2, S, hd), BF16),
                pltpu.VMEM(tile, F32),
                pltpu.VMEM(tile if not band else (8, 128), F32),
                pltpu.VMEM(tile, BF16),
                pltpu.VMEM((2, S, hd) if band else (2, 8, hd), F32),
                pltpu.VMEM((2, n, r, hd), BF16),
                pltpu.VMEM((2, n, r, hd), BF16),
                pltpu.VMEM(streams, BF16),
                pltpu.VMEM(streams, BF16),
                pltpu.VMEM((2, far_rows, 2 * hd), BF16),
                pltpu.VMEM((2, r, 2 * hd), BF16),
                pltpu.VMEM((r, 2 * hd), BF16),
                pltpu.VMEM((r, width), F32),
                pltpu.VMEM((2, r, hd), BF16),
                pltpu.VMEM((S,), jnp.int32),
            ],
            compiler_params=pltpu.CompilerParams(
                collective_id=0, has_side_effects=True, vmem_limit_bytes=60 * 1024 * 1024
            ),
        )(
            inputs,
            key_weight,
            value_weight,
            queries,
            output_cotangent,
            documents,
        )
        return pl.pallas_call(
            write_kernel,
            out_shape=(
                jax.ShapeDtypeStruct(query_grad.shape, BF16),
                jax.ShapeDtypeStruct(input_grad.shape, BF16),
            ),
            in_specs=[vmem] * 2,
            out_specs=(anywhere, anywhere),
            scratch_shapes=[dma((2,))],
            compiler_params=pltpu.CompilerParams(vmem_limit_bytes=1024 * 1024),
        )(query_grad, input_grad)

    placed = (
        P(("layer", "qblk"), None),
        P(None, "head"),
        P(None, "head"),
        P("layer", "qblk", "head"),
        P("layer", "qblk", "head"),
        P(),
    )
    return jax.shard_map(
        local,
        mesh=mesh,
        in_specs=placed,
        out_specs=(P("layer", "qblk", "head"), P(("layer", "qblk"), "head")),
        check_vma=False,
    )
```
